256 devices in a mesh: dp: 32 (over x, y, core), tensor: 8 (over z).
Axes of the slice: x: 4, y: 4, z: 8, core: 2. Of those that a mesh axis runs over, the one named last changes fastest.
Arguments:
- queries: bfloat16 [1536, 5, 8192], P('dp', None, 'tensor'), may hold values from -6 to 6
- new_keys: bfloat16 [1536, 5, 1024], P('dp', None, 'tensor'), may hold values from -6 to 6
- new_values: bfloat16 [1536, 5, 1024], P('dp', None, 'tensor'), may hold values from -6 to 6
- key_cache: bfloat16 [1536, 256, 1024], P('dp', None, 'tensor'), may hold values from -6 to 6
- value_cache: bfloat16 [1536, 256, 1024], P('dp', None, 'tensor'), may hold values from -6 to 6
- cache_lengths: int32 [1536], P('dp'), may hold values from 2 to 256, as said below
- accepted: int32 [1536], P('dp'), may hold values from 0 to 4
- head_weight: bfloat16 [8192, 32768], P('tensor', 'dp'), may hold values from -1.3203125 to 1.3203125
Outputs:
- drafter_logits: float32 [1536, 32768], P('tensor', 'dp')
The draws below stay inside these ranges and needn't reach their ends.
Inputs may be any that keep to these rules, and one draw needn't show every extreme that they name: `cache_lengths`: row 0 holds 256 valid slots.
All inputs are finite; a program needn't handle non-finite values.
Results may differ from the reference program's by a relative error of at most 0.015.
Values may be sent and summed in bfloat16 or wider, within the bound.
A program may use at most 128 MiB of HBM per device.

```python
import jax
import jax.numpy as jnp
from jax import lax

D = 8192
HEADS = 64
KV_HEADS = 8
HEAD_DIM = 128
VOCAB = 32768
DRAFT = 5
ROWS_DEV = 48
CACHE = 256
ROWS = 1536
N_TENSOR = 8


def draw_queries(key, part):
    values = jnp.clip(jax.random.normal(jax.random.fold_in(key, 1), (ROWS, DRAFT, D)), -6.0, 6.0)
    return values.astype(jnp.bfloat16)


def draw_key_cache(key, part):
    values = jnp.clip(jax.random.normal(jax.random.fold_in(key, 2), (ROWS, CACHE, KV_HEADS * HEAD_DIM)), -6.0, 6.0)
    return values.astype(jnp.bfloat16)


def draw_cache_lengths(key, part):
    base = jax.random.randint(jax.random.fold_in(key, 5), (ROWS,), 0, CACHE - 1)
    factor = jax.random.randint(jax.random.fold_in(key, 6), (ROWS // ROWS_DEV,), 1, 5)
    factor = jnp.repeat(factor, ROWS_DEV)
    lengths = 2 + base * factor // 4
    return lengths.at[0].set(CACHE).astype(jnp.int32)


def set_ends(result, own_key, smallest, largest):
    spot = [jax.random.randint(jax.random.fold_in(own_key, axis), (), 0, length) for axis, length in enumerate(result.shape)]
    longest = result.shape.index(max(result.shape))
    beside = spot[:longest] + [(spot[longest] + 1) % result.shape[longest]] + spot[longest + 1:]
    return result.at[tuple(spot)].set(smallest).at[tuple(beside)].set(largest)


def shard_levels(stream_key, dims, pieces, smallest, high):
    level, own = 1.0, jax.random.fold_in(stream_key, 6)
    for dim, blocks in pieces:
        draws = jnp.exp(jax.random.uniform(jax.random.fold_in(own, dim), (blocks,), jnp.float32, smallest / len(pieces), high / len(pieces)))
        level = level * jnp.repeat(draws, dims[dim] // blocks).reshape([-1 if axis == dim else 1 for axis in range(len(dims))])
    return level


def noise(own_key, dims, width, bound, cuts=(), held_as=jnp.bfloat16):
    level = shard_levels(own_key, dims, cuts, -0.22, 0.18) if cuts else 1.0
    values = jax.random.normal(own_key, dims, jnp.float32) * width * level
    return jnp.minimum(jnp.maximum(values, -bound), bound).astype(held_as)


def setup_inputs(seed: int = 0) -> dict:
    streams_of = jax.random.split(jax.random.key(seed), 9)
    queries = draw_queries(jax.random.fold_in(streams_of[8], 71), 0)
    new_keys = noise(streams_of[1], (ROWS, DRAFT, KV_HEADS * HEAD_DIM), 1.0, 6.0, ((0, 32), (2, 8)))
    new_values = noise(streams_of[2], (ROWS, DRAFT, KV_HEADS * HEAD_DIM), 1.0, 6.0, ((0, 32), (2, 8)))
    key_cache = draw_key_cache(jax.random.fold_in(streams_of[8], 71), 0)
    value_cache = noise(streams_of[4], (ROWS, CACHE, KV_HEADS * HEAD_DIM), 1.0, 6.0, ((0, 32), (2, 8)))
    cache_lengths = draw_cache_lengths(jax.random.fold_in(streams_of[8], 71), 0)
    accepted = set_ends(jax.random.randint(streams_of[6], (ROWS,), 0, DRAFT), jax.random.fold_in(streams_of[6], 1), 0, DRAFT - 1).astype(jnp.int32)
    head_weight = noise(streams_of[7], (D, VOCAB), (20.0 * D ** -0.5), 1.3203125, ((0, 8), (1, 32)))
    return {"queries": queries, "new_keys": new_keys, "new_values": new_values, "key_cache": key_cache, "value_cache": value_cache, "cache_lengths": cache_lengths, "accepted": accepted, "head_weight": head_weight}


def verify(queries, new_keys, new_values, key_cache, value_cache, cache_lengths):
    row_count = queries.shape[0]
    sharing = HEADS // KV_HEADS
    query_heads = queries.astype(jnp.float32).reshape(row_count, DRAFT, KV_HEADS, sharing, HEAD_DIM)
    past_keys = key_cache.astype(jnp.float32).reshape(row_count, CACHE, KV_HEADS, HEAD_DIM)
    past_values = value_cache.astype(jnp.float32).reshape(row_count, CACHE, KV_HEADS, HEAD_DIM)
    fresh_keys = new_keys.astype(jnp.float32).reshape(row_count, DRAFT, KV_HEADS, HEAD_DIM)
    fresh_values = new_values.astype(jnp.float32).reshape(row_count, DRAFT, KV_HEADS, HEAD_DIM)
    scaling = HEAD_DIM ** -0.5
    past_scores = jnp.einsum("bpgjd,blgd->bpgjl", query_heads, past_keys) * scaling
    fresh_scores = jnp.einsum("bpgjd,bqgd->bpgjq", query_heads, fresh_keys) * scaling
    past_mask = (jnp.arange(CACHE, dtype=jnp.int32)[None, :] < cache_lengths[:, None])[:, None, None, None, :]
    fresh_mask = (jnp.arange(DRAFT)[None, :] <= jnp.arange(DRAFT)[:, None])[None, :, None, None, :]
    lowest = -1e30
    past_masked = jnp.where(past_mask, past_scores, lowest)
    fresh_masked = jnp.where(fresh_mask, fresh_scores, lowest)
    peaks = jnp.maximum(jnp.max(past_masked, axis=-1, keepdims=True), jnp.max(fresh_masked, axis=-1, keepdims=True))
    past_exp = jnp.exp(past_masked - peaks)
    fresh_exp = jnp.exp(fresh_masked - peaks)
    totals = jnp.sum(past_exp, axis=-1, keepdims=True) + jnp.sum(fresh_exp, axis=-1, keepdims=True)
    past_weights = lax.optimization_barrier((past_exp / totals).astype(jnp.bfloat16)).astype(jnp.float32)
    fresh_weights = lax.optimization_barrier((fresh_exp / totals).astype(jnp.bfloat16)).astype(jnp.float32)
    mixed = jnp.einsum("bpgjl,blgd->bpgjd", past_weights, past_values)
    mixed = mixed + jnp.einsum("bpgjq,bqgd->bpgjd", fresh_weights, fresh_values)
    return mixed.astype(jnp.bfloat16).reshape(row_count, DRAFT, D)


def reference(queries, new_keys, new_values, key_cache, value_cache, cache_lengths, accepted, head_weight):
    blocks = ROWS // ROWS_DEV

    def stacked(array):
        return array.reshape((blocks, ROWS_DEV) + array.shape[1:])

    def one_block(inputs):
        return verify(*inputs)

    attended = lax.map(one_block, (stacked(queries), stacked(new_keys), stacked(new_values), stacked(key_cache), stacked(value_cache), stacked(cache_lengths)))
    attended = attended.reshape(ROWS, DRAFT, D)
    picked = jnp.take_along_axis(attended, accepted.astype(jnp.int32)[:, None, None], axis=1)[:, 0, :]
    slices = picked.reshape(ROWS, N_TENSOR, D // N_TENSOR)
    head_parts = head_weight.reshape(N_TENSOR, D // N_TENSOR, VOCAB)

    def add_part(shard, total):
        features = lax.dynamic_index_in_dim(slices, shard, 1, keepdims=False)
        weights = lax.dynamic_index_in_dim(head_parts, shard, 0, keepdims=False)
        part = jnp.dot(features, weights, preferred_element_type=jnp.float32)
        part = lax.optimization_barrier(part.astype(jnp.bfloat16))
        return total + part.astype(jnp.float32)

    return lax.fori_loop(0, N_TENSOR, add_part, jnp.zeros((ROWS, VOCAB), jnp.float32))
```

```python
import jax
import jax.numpy as jnp
from jax import lax
from jax.sharding import PartitionSpec as P

HEAD_DIM = 128


def attend(queries, new_keys, new_values, key_cache, value_cache, cache_lengths, accepted):
    rows, draft, cols = queries.shape
    cache = key_cache.shape[1]
    heads = cols // HEAD_DIM
    spot = jnp.arange(draft, dtype=jnp.int32)[None, :]
    chosen = spot == accepted[:, None]
    query = jnp.sum(jnp.where(chosen[:, :, None], queries, 0).astype(jnp.float32), axis=1)
    query = query.astype(jnp.bfloat16).reshape(rows, heads, HEAD_DIM)
    scale = HEAD_DIM ** -0.5
    past = jnp.einsum("bjd,bld->bjl", query, key_cache, preferred_element_type=jnp.float32) * scale
    fresh = jnp.einsum("bjd,bqd->bjq", query, new_keys, preferred_element_type=jnp.float32) * scale
    past_ok = jnp.arange(cache, dtype=jnp.int32)[None, :] < cache_lengths[:, None]
    past = jnp.where(past_ok[:, None, :], past, -1e30)
    fresh = jnp.where((spot <= accepted[:, None])[:, None, :], fresh, -1e30)
    peak = jnp.maximum(jnp.max(past, -1, keepdims=True), jnp.max(fresh, -1, keepdims=True))
    past, fresh = jnp.exp(past - peak), jnp.exp(fresh - peak)
    total = jnp.sum(past, -1, keepdims=True) + jnp.sum(fresh, -1, keepdims=True)
    past, fresh = (past / total).astype(jnp.bfloat16), (fresh / total).astype(jnp.bfloat16)
    mixed = jnp.einsum("bjl,bld->bjd", past, value_cache, preferred_element_type=jnp.float32)
    mixed = mixed + jnp.einsum("bjq,bqd->bjd", fresh, new_values, preferred_element_type=jnp.float32)
    return mixed.astype(jnp.bfloat16).reshape(rows, cols)


def shards(queries, new_keys, new_values, key_cache, value_cache, cache_lengths, accepted, head_weight):
    picked = attend(queries, new_keys, new_values, key_cache, value_cache, cache_lengths, accepted)
    everything = lax.all_gather(picked, "dp", axis=0, tiled=True)
    part = jnp.dot(everything, head_weight, preferred_element_type=jnp.float32).astype(jnp.bfloat16)
    return lax.psum_scatter(part, "tensor", scatter_dimension=0, tiled=True).astype(jnp.float32)


def solution(mesh):
    split = P("dp", None, "tensor")
    return jax.shard_map(
        shards,
        mesh=mesh,
        in_specs=(split,) * 5 + (P("dp"), P("dp"), P("tensor", "dp")),
        out_specs=P("tensor", "dp"),
        check_vma=False,
    )
```

```python
import functools

import jax
import jax.numpy as jnp
from jax import lax
from jax.experimental import pallas as pl
from jax.experimental.pallas import tpu as pltpu
from jax.sharding import PartitionSpec as P

HEAD_DIM = 128
MESH = pl.DeviceIdType.MESH
SLOTS = 14
div, rem = lax.div, lax.rem


def attend(queries, new_keys, new_values, key_cache, value_cache, cache_lengths, accepted):
    rows, draft, cols = queries.shape
    cache = key_cache.shape[1]
    heads = cols // HEAD_DIM
    spot = jnp.arange(draft, dtype=jnp.int32)[None, :]
    chosen = spot == accepted[:, None]
    query = jnp.sum(jnp.where(chosen[:, :, None], queries, 0).astype(jnp.float32), axis=1)
    query = query.astype(jnp.bfloat16).reshape(rows, heads, HEAD_DIM)
    scale = HEAD_DIM ** -0.5
    past = jnp.einsum("bjd,bld->bjl", query, key_cache, preferred_element_type=jnp.float32) * scale
    fresh = jnp.einsum("bjd,bqd->bjq", query, new_keys, preferred_element_type=jnp.float32) * scale
    past_ok = jnp.arange(cache, dtype=jnp.int32)[None, :] < cache_lengths[:, None]
    past = jnp.where(past_ok[:, None, :], past, -1e30)
    fresh = jnp.where((spot <= accepted[:, None])[:, None, :], fresh, -1e30)
    peak = jnp.maximum(jnp.max(past, -1, keepdims=True), jnp.max(fresh, -1, keepdims=True))
    past, fresh = jnp.exp(past - peak), jnp.exp(fresh - peak)
    total = jnp.sum(past, -1, keepdims=True) + jnp.sum(fresh, -1, keepdims=True)
    past, fresh = (past / total).astype(jnp.bfloat16), (fresh / total).astype(jnp.bfloat16)
    mixed = jnp.einsum("bjl,bld->bjd", past, value_cache, preferred_element_type=jnp.float32)
    mixed = mixed + jnp.einsum("bjq,bqd->bjd", fresh, new_values, preferred_element_type=jnp.float32)
    return mixed.astype(jnp.bfloat16).reshape(rows, cols)


def exchange(picked_hbm, weight_hbm, out_hbm, feats, weight, up_in, up_out, dn_in, dn_out, total,
             load_sem, feat_sem, line_sem, cross_sem, swap_sem, up_sem, dn_sem, up_got, dn_got, store_sem):
    dp, z = lax.axis_index("dp"), lax.axis_index("tensor")
    core, chip = rem(dp, 2), div(dp, 2)
    x, y = div(chip, 4), rem(chip, 4)
    across = 1 - core

    def line_peer(k):
        return (rem(x + k * across, 4) * 4 + rem(y + k * core, 4)) * 2 + core

    def cross_peer(k):
        return (rem(x + k * core, 4) * 4 + rem(y + k * across, 4)) * 2 + core

    partner = chip * 2 + across
    above, below = (dp, rem(z + 1, 8)), (dp, rem(z + 7, 8))
    peers = [(line_peer(k), z) for k in (1, 2, 3)] + [(cross_peer(k), z) for k in (1, 2, 3)]
    peers += [(partner, z), above, below]

    loads = [pltpu.make_async_copy(picked_hbm, feats.at[dp], load_sem.at[2])]
    loads += [pltpu.make_async_copy(weight_hbm.at[:, pl.ds(512 * h, 512)], weight.at[h], load_sem.at[h]) for h in range(2)]
    for load in loads:
        load.start()

    barrier = pltpu.get_barrier_semaphore()
    for peer in peers:
        pl.semaphore_signal(barrier, inc=1, device_id=peer, device_id_type=MESH)
    pl.semaphore_wait(barrier, len(peers))
    loads[0].wait()

    def give(shard, to, sent):
        return pltpu.make_async_remote_copy(
            src_ref=feats.at[shard], dst_ref=feats.at[shard], send_sem=sent, recv_sem=feat_sem.at[shard],
            device_id=(to, z), device_id_type=MESH)

    def take(shard):
        give(shard, partner, swap_sem.at[0]).wait_recv()

    for k in (1, 3, 2):
        give(dp, line_peer(k), line_sem.at[k - 1]).start()
    give(dp, partner, swap_sem.at[chip]).start()

    odd = rem(div(y, 2) + z, 2)
    late = div(rem(2 * x + 12 - z, 8), 4)
    for i, (even_e, odd_e) in enumerate(((0, 1), (2, 7), (6, 3), (4, 5))):
        block = rem(z + 4 + even_e + (odd_e - even_e) * odd, 8)
        member = across * (div(block, 2) * 4 + y) + core * (x * 4 + 2 * rem(late + i // 2, 2) + i % 2)
        shard = member * 2 + core

        @pl.when(member != chip)
        def _():
            take(shard)
            give(shard, partner, swap_sem.at[member]).start()

        for k in (1, 3, 2):
            give(shard, cross_peer(k), cross_sem.at[i, k - 1]).start()

    def pass_on(block):
        for p in range(2):
            member = 2 * block + p
            inside = across * (rem(member, 4) - y) + core * (div(member, 4) - x)

            @pl.when(inside != 0)
            def _():
                take(member * 2 + core)
                give(member * 2 + core, partner, swap_sem.at[member]).start()

    def receive(block):
        for p in range(2):
            take((2 * block + p) * 2 + across)

    def send(n, goes_up):
        source, target = (up_out, up_in) if goes_up else (dn_out, dn_in)
        sent, got = (up_sem, up_got) if goes_up else (dn_sem, dn_got)
        return pltpu.make_async_remote_copy(
            src_ref=source.at[n], dst_ref=target.at[n], send_sem=sent.at[n], recv_sem=got.at[n],
            device_id=above if goes_up else below, device_id_type=MESH)

    def product(chip_a, chip_b, h):
        a = feats[pl.ds(2 * chip_a, 2)].reshape(96, 1024)
        b = feats[pl.ds(2 * chip_b, 2)].reshape(96, 1024)
        return jnp.dot(jnp.concatenate([a, b], axis=0), weight[h], preferred_element_type=jnp.float32)

    def slot(n, has_input):
        m = n + 2
        j = 4 - div(m, 4)
        q, h = rem(div(m, 2), 2), rem(m, 2)
        up_block, dn_block = rem(z + j, 8), rem(z + 8 - j, 8)

        @pl.when(jnp.logical_or(n == 0, rem(n, 4) == 2))
        def _():
            pass_on(up_block)

            @pl.when(n > 0)
            def _():
                pass_on(dn_block)

            receive(up_block)

            @pl.when(n > 0)
            def _():
                receive(dn_block)

        sums = product(2 * up_block + 1 - q, 2 * dn_block + q, h)
        up, dn = sums[:96], sums[96:]
        if has_input:
            send(n - 4, True).wait_recv()
            up = up + up_in[n - 4].astype(jnp.float32)
        up_out[n] = up.astype(jnp.bfloat16)
        send(n, True).start()
        if has_input:
            send(n - 4, False).wait_recv()
            dn = dn + dn_in[n - 4].astype(jnp.float32)
        dn_out[n] = dn.astype(jnp.bfloat16)
        send(n, False).start()

    for load in loads[1:]:
        load.wait()

    def start_slot(n, carry):
        slot(n, False)
        return carry

    def inner_slot(n, carry):
        slot(n, True)
        return carry

    lax.fori_loop(0, 4, start_slot, 0)
    lax.fori_loop(4, SLOTS, inner_slot, 0)

    pass_on(z)
    receive(z)
    for h in range(2):
        sums = product(2 * z, 2 * z + 1, h)
        total[0, h] = sums[:96]
        total[1, h] = sums[96:]
    for h in range(2):
        send(10 + h, True).wait_recv()
        total[1, h] = total[1, h] + up_in[10 + h].astype(jnp.float32)
        send(10 + h, False).wait_recv()
        total[0, h] = total[0, h] + dn_in[10 + h].astype(jnp.float32)
    stores = []
    for h in range(2):
        for p in range(2):
            send(12 + h, p == 0).wait_recv()
            last = (up_in if p == 0 else dn_in)[12 + h]
            total[p, h] = total[p, h] + last.astype(jnp.float32)
            stores.append(pltpu.make_async_copy(
                total.at[p, h], out_hbm.at[pl.ds(96 * p, 96), pl.ds(512 * h, 512)], store_sem.at[p, h]))
            stores[-1].start()

    for k in (1, 2, 3):
        give(dp, partner, line_sem.at[k - 1]).wait_send()
    for i in range(4):
        for k in (1, 2, 3):
            give(dp, partner, cross_sem.at[i, k - 1]).wait_send()

    def drain_swap(i, carry):
        give(dp, partner, swap_sem.at[i]).wait_send()
        return carry

    def drain(n, carry):
        send(n, True).wait_send()
        send(n, False).wait_send()
        return carry

    lax.fori_loop(0, 16, drain_swap, 0)
    lax.fori_loop(0, SLOTS, drain, 0)
    for store in stores:
        store.wait()


def head(picked, head_weight):
    dma = pltpu.SemaphoreType.DMA
    piece = pltpu.VMEM((SLOTS, 96, 512), jnp.bfloat16)
    return pl.pallas_call(
        exchange,
        out_shape=jax.ShapeDtypeStruct((192, 1024), jnp.float32),
        in_specs=[pl.BlockSpec(memory_space=pl.ANY)] * 2,
        out_specs=pl.BlockSpec(memory_space=pl.ANY),
        scratch_shapes=[
            pltpu.VMEM((32, 48, 1024), jnp.bfloat16),
            pltpu.VMEM((2, 1024, 512), jnp.bfloat16),
            piece, piece, piece, piece,
            pltpu.VMEM((2, 2, 96, 512), jnp.float32),
            dma((3,)), dma((32,)), dma((3,)), dma((4, 3)), dma((16,)),
            dma((SLOTS,)), dma((SLOTS,)), dma((SLOTS,)), dma((SLOTS,)), dma((2, 2)),
        ],
        compiler_params=pltpu.CompilerParams(
            collective_id=0, has_side_effects=True, vmem_limit_bytes=40 * 2 ** 20),
    )(picked, head_weight)


def shards(queries, new_keys, new_values, key_cache, value_cache, cache_lengths, accepted, head_weight):
    picked = attend(queries, new_keys, new_values, key_cache, value_cache, cache_lengths, accepted)
    return head(picked, head_weight)


def solution(mesh):
    split = P("dp", None, "tensor")
    return jax.shard_map(
        shards,
        mesh=mesh,
        in_specs=(split,) * 5 + (P("dp"), P("dp"), P("tensor", "dp")),
        out_specs=P("tensor", "dp"),
        check_vma=False,
    )
```

```python
import jax
import jax.numpy as jnp
from jax import lax
from jax.experimental import pallas as pl
from jax.experimental.pallas import tpu as pltpu
from jax.sharding import PartitionSpec as P

HEAD_DIM = 128
MESH = pl.DeviceIdType.MESH
SLOTS = 14
div, rem = lax.div, lax.rem


def attend_rows(step, queries, new_keys, new_values, keys, values, lengths, accepted, out):
    scale = HEAD_DIM ** -0.5
    row = lax.broadcasted_iota(jnp.int32, (8, 128), 0)
    lane = lax.broadcasted_iota(jnp.int32, (8, 128), 1)
    row_wide = lax.broadcasted_iota(jnp.int32, (8, 256), 0)
    lane_wide = lax.broadcasted_iota(jnp.int32, (8, 256), 1)
    blank = jnp.zeros((128 - 5 * 8, HEAD_DIM), jnp.float32)
    base = pl.multiple_of(16 * step, 16)
    span = pl.ds(base, 16)

    def heads(tile):
        return jnp.concatenate([tile] * 8, axis=0)

    attended = []
    for part in range(2):
        start, some = base + 8 * part, slice(8 * part, 8 * part + 8)
        choice = jnp.zeros((8, 128), jnp.int32)
        length = jnp.zeros((8, 256), jnp.int32)
        for i in range(8):
            choice = jnp.where(row == i, accepted[start + i], choice)
            length = jnp.where(row_wide == i, lengths[start + i], length)
        choices = jnp.concatenate([choice] * 8, axis=1)
        query = jnp.zeros((8, 1024), jnp.float32)
        for p in range(5):
            query = jnp.where(choices == p, queries[p, span, :].astype(jnp.float32)[some], query)
        query = jnp.concatenate([query[:, 128 * h:128 * h + 128] for h in range(8)], axis=0).astype(jnp.bfloat16)

        def fresh_rows(ref):
            parts = [ref[p, span, :].astype(jnp.float32)[some] for p in range(5)]
            return jnp.concatenate(parts + [blank], axis=0).astype(jnp.bfloat16)

        def scores(block):
            return lax.dot_general(query, block, (((1,), (1,)), ((), ())), preferred_element_type=jnp.float32)

        own_row = heads(row_wide)
        past = scores(keys[start])
        for i in range(1, 8):
            past = jnp.where(own_row == i, scores(keys[start + i]), past)
        past = jnp.where(heads(lane_wide < length), past * scale, -1e30)
        fresh_ok = (lane % 8 == row) & (lane // 8 <= choice) & (lane < 40)
        fresh = jnp.where(heads(fresh_ok), scores(fresh_rows(new_keys)) * scale, -1e30)
        peak = jnp.maximum(jnp.max(past, -1, keepdims=True), jnp.max(fresh, -1, keepdims=True))
        past, fresh = jnp.exp(past - peak), jnp.exp(fresh - peak)
        share = 1.0 / (jnp.sum(past, -1, keepdims=True) + jnp.sum(fresh, -1, keepdims=True))
        past, fresh = (past * share).astype(jnp.bfloat16), (fresh * share).astype(jnp.bfloat16)
        own_row = heads(row)
        mixed = jnp.dot(past, values[start], preferred_element_type=jnp.float32)
        for i in range(1, 8):
            mixed = jnp.where(own_row == i, jnp.dot(past, values[start + i], preferred_element_type=jnp.float32), mixed)
        mixed = mixed + jnp.dot(fresh, fresh_rows(new_values), preferred_element_type=jnp.float32)
        attended.append(jnp.concatenate([mixed[8 * h:8 * h + 8] for h in range(8)], axis=1))
    out[span, :] = jnp.concatenate(attended, axis=0).astype(jnp.bfloat16)


def exchange(lengths, accepted, queries_hbm, new_keys_hbm, new_values_hbm, keys_hbm, values_hbm, weight_hbm, out_hbm,
             queries, new_keys, new_values, keys, values, feats, weight, up_in, up_out, dn_in, dn_out, total,
             small_sem, cache_sem, load_sem, feat_sem, line_sem, cross_sem, swap_sem, up_sem, dn_sem, up_got, dn_got, store_sem):
    dp, z = lax.axis_index("dp"), lax.axis_index("tensor")
    core, chip = rem(dp, 2), div(dp, 2)
    x, y = div(chip, 4), rem(chip, 4)
    across = 1 - core

    def line_peer(k):
        return (rem(x + k * across, 4) * 4 + rem(y + k * core, 4)) * 2 + core

    def cross_peer(k):
        return (rem(x + k * core, 4) * 4 + rem(y + k * across, 4)) * 2 + core

    partner = chip * 2 + across
    above, below = (dp, rem(z + 1, 8)), (dp, rem(z + 7, 8))
    peers = [(line_peer(k), z) for k in (1, 2, 3)] + [(cross_peer(k), z) for k in (1, 2, 3)]
    peers += [(partner, z), above, below]

    smalls = [pltpu.make_async_copy(source, target, small_sem.at[i]) for i, (source, target) in enumerate(
        ((queries_hbm, queries), (new_keys_hbm, new_keys), (new_values_hbm, new_values)))]

    def cache_load(step, which):
        source, target = ((keys_hbm, keys), (values_hbm, values))[which]
        span = pl.ds(16 * step, 16)
        return pltpu.make_async_copy(source.at[span], target.at[span], cache_sem.at[which, step])

    caches = [cache_load(step, which) for step in range(3) for which in range(2)]
    loads = [pltpu.make_async_copy(weight_hbm.at[:, pl.ds(512 * h, 512)], weight.at[h], load_sem.at[h]) for h in range(2)]
    for load in smalls + caches + loads:
        load.start()

    barrier = pltpu.get_barrier_semaphore()
    for peer in peers:
        pl.semaphore_signal(barrier, inc=1, device_id=peer, device_id_type=MESH)

    for load in smalls:
        load.wait()

    def attend_step(step, carry):
        cache_load(step, 0).wait()
        cache_load(step, 1).wait()
        attend_rows(step, queries, new_keys, new_values, keys, values, lengths, accepted, feats.at[dp])
        return carry

    lax.fori_loop(0, 3, attend_step, 0)
    pl.semaphore_wait(barrier, len(peers))

    def give(shard, to, sent):
        return pltpu.make_async_remote_copy(
            src_ref=feats.at[shard], dst_ref=feats.at[shard], send_sem=sent, recv_sem=feat_sem.at[shard],
            device_id=(to, z), device_id_type=MESH)

    def take(shard):
        give(shard, partner, swap_sem.at[0]).wait_recv()

    for k in (1, 3, 2):
        give(dp, line_peer(k), line_sem.at[k - 1]).start()
    give(dp, partner, swap_sem.at[chip]).start()

    odd = rem(div(y, 2) + z, 2)
    late = div(rem(2 * x + 12 - z, 8), 4)
    for i, (even_e, odd_e) in enumerate(((0, 1), (2, 7), (6, 3), (4, 5))):
        block = rem(z + 4 + even_e + (odd_e - even_e) * odd, 8)
        member = across * (div(block, 2) * 4 + y) + core * (x * 4 + 2 * rem(late + i // 2, 2) + i % 2)
        shard = member * 2 + core

        @pl.when(member != chip)
        def _():
            take(shard)
            give(shard, partner, swap_sem.at[member]).start()

        for k in (1, 3, 2):
            give(shard, cross_peer(k), cross_sem.at[i, k - 1]).start()

    def pass_on(block):
        for p in range(2):
            member = 2 * block + p
            inside = across * (rem(member, 4) - y) + core * (div(member, 4) - x)

            @pl.when(inside != 0)
            def _():
                take(member * 2 + core)
                give(member * 2 + core, partner, swap_sem.at[member]).start()

    def receive(block):
        for p in range(2):
            take((2 * block + p) * 2 + across)

    def send(n, goes_up):
        source, target = (up_out, up_in) if goes_up else (dn_out, dn_in)
        sent, got = (up_sem, up_got) if goes_up else (dn_sem, dn_got)
        return pltpu.make_async_remote_copy(
            src_ref=source.at[n], dst_ref=target.at[n], send_sem=sent.at[n], recv_sem=got.at[n],
            device_id=above if goes_up else below, device_id_type=MESH)

    def product(chip_a, chip_b, h):
        a = feats[pl.ds(2 * chip_a, 2)].reshape(96, 1024)
        b = feats[pl.ds(2 * chip_b, 2)].reshape(96, 1024)
        return jnp.dot(jnp.concatenate([a, b], axis=0), weight[h], preferred_element_type=jnp.float32)

    def slot(n, has_input):
        m = n + 2
        j = 4 - div(m, 4)
        q, h = rem(div(m, 2), 2), rem(m, 2)
        up_block, dn_block = rem(z + j, 8), rem(z + 8 - j, 8)

        @pl.when(jnp.logical_or(n == 0, rem(n, 4) == 2))
        def _():
            pass_on(up_block)

            @pl.when(n > 0)
            def _():
                pass_on(dn_block)

            receive(up_block)

            @pl.when(n > 0)
            def _():
                receive(dn_block)

        sums = product(2 * up_block + 1 - q, 2 * dn_block + q, h)
        up, dn = sums[:96], sums[96:]
        if has_input:
            send(n - 4, True).wait_recv()
            up = up + up_in[n - 4].astype(jnp.float32)
        up_out[n] = up.astype(jnp.bfloat16)
        send(n, True).start()
        if has_input:
            send(n - 4, False).wait_recv()
            dn = dn + dn_in[n - 4].astype(jnp.float32)
        dn_out[n] = dn.astype(jnp.bfloat16)
        send(n, False).start()

    for load in loads:
        load.wait()

    def start_slot(n, carry):
        slot(n, False)
        return carry

    def inner_slot(n, carry):
        slot(n, True)
        return carry

    lax.fori_loop(0, 4, start_slot, 0)
    lax.fori_loop(4, SLOTS, inner_slot, 0)

    pass_on(z)
    receive(z)
    for h in range(2):
        sums = product(2 * z, 2 * z + 1, h)
        total[0, h] = sums[:96]
        total[1, h] = sums[96:]
    for h in range(2):
        send(10 + h, True).wait_recv()
        total[1, h] = total[1, h] + up_in[10 + h].astype(jnp.float32)
        send(10 + h, False).wait_recv()
        total[0, h] = total[0, h] + dn_in[10 + h].astype(jnp.float32)
    stores = []
    for h in range(2):
        for p in range(2):
            send(12 + h, p == 0).wait_recv()
            last = (up_in if p == 0 else dn_in)[12 + h]
            total[p, h] = total[p, h] + last.astype(jnp.float32)
            stores.append(pltpu.make_async_copy(
                total.at[p, h], out_hbm.at[pl.ds(96 * p, 96), pl.ds(512 * h, 512)], store_sem.at[p, h]))
            stores[-1].start()

    for k in (1, 2, 3):
        give(dp, partner, line_sem.at[k - 1]).wait_send()
    for i in range(4):
        for k in (1, 2, 3):
            give(dp, partner, cross_sem.at[i, k - 1]).wait_send()

    def drain_swap(i, carry):
        give(dp, partner, swap_sem.at[i]).wait_send()
        return carry

    def drain(n, carry):
        send(n, True).wait_send()
        send(n, False).wait_send()
        return carry

    lax.fori_loop(0, 16, drain_swap, 0)
    lax.fori_loop(0, SLOTS, drain, 0)
    for store in stores:
        store.wait()


def shards(queries, new_keys, new_values, key_cache, value_cache, cache_lengths, accepted, head_weight):
    dma = pltpu.SemaphoreType.DMA
    piece = pltpu.VMEM((SLOTS, 96, 512), jnp.bfloat16)
    queries, new_keys, new_values = (jnp.transpose(a, (1, 0, 2)) for a in (queries, new_keys, new_values))
    return pl.pallas_call(
        exchange,
        out_shape=jax.ShapeDtypeStruct((192, 1024), jnp.float32),
        in_specs=[pl.BlockSpec(memory_space=pltpu.SMEM)] * 2 + [pl.BlockSpec(memory_space=pl.ANY)] * 6,
        out_specs=pl.BlockSpec(memory_space=pl.ANY),
        scratch_shapes=[
            pltpu.VMEM((5, 48, 1024), jnp.bfloat16),
            pltpu.VMEM((5, 48, 128), jnp.bfloat16),
            pltpu.VMEM((5, 48, 128), jnp.bfloat16),
            pltpu.VMEM((48, 256, 128), jnp.bfloat16),
            pltpu.VMEM((48, 256, 128), jnp.bfloat16),
            pltpu.VMEM((32, 48, 1024), jnp.bfloat16),
            pltpu.VMEM((2, 1024, 512), jnp.bfloat16),
            piece, piece, piece, piece,
            pltpu.VMEM((2, 2, 96, 512), jnp.float32),
            dma((3,)), dma((2, 3)), dma((2,)), dma((32,)), dma((3,)), dma((4, 3)), dma((16,)),
            dma((SLOTS,)), dma((SLOTS,)), dma((SLOTS,)), dma((SLOTS,)), dma((2, 2)),
        ],
        compiler_params=pltpu.CompilerParams(
            collective_id=0, has_side_effects=True, vmem_limit_bytes=54 * 2 ** 20),
    )(cache_lengths, accepted, queries, new_keys, new_values, key_cache, value_cache, head_weight)


def solution(mesh):
    split = P("dp", None, "tensor")
    return jax.shard_map(
        shards,
        mesh=mesh,
        in_specs=(split,) * 5 + (P("dp"), P("dp"), P("tensor", "dp")),
        out_specs=P("tensor", "dp"),
        check_vma=False,
    )
```

```python
import jax
import jax.numpy as jnp
from jax import lax
from jax.experimental import pallas as pl
from jax.experimental.pallas import tpu as pltpu
from jax.sharding import PartitionSpec as P

HEAD_DIM = 128
MESH = pl.DeviceIdType.MESH
SLOTS = 21
div, rem = lax.div, lax.rem


def attend_rows(step, queries, new_keys, new_values, keys, values, lengths, accepted, out):
    scale = HEAD_DIM ** -0.5
    row = lax.broadcasted_iota(jnp.int32, (8, 128), 0)
    lane = lax.broadcasted_iota(jnp.int32, (8, 128), 1)
    row_wide = lax.broadcasted_iota(jnp.int32, (8, 256), 0)
    lane_wide = lax.broadcasted_iota(jnp.int32, (8, 256), 1)
    blank = jnp.zeros((128 - 5 * 8, HEAD_DIM), jnp.float32)
    base = pl.multiple_of(16 * step, 16)
    span = pl.ds(base, 16)

    def heads(tile):
        return jnp.concatenate([tile] * 8, axis=0)

    attended = []
    for part in range(2):
        start, some = base + 8 * part, slice(8 * part, 8 * part + 8)
        choice = jnp.zeros((8, 128), jnp.int32)
        length = jnp.zeros((8, 256), jnp.int32)
        for i in range(8):
            choice = jnp.where(row == i, accepted[start + i], choice)
            length = jnp.where(row_wide == i, lengths[start + i], length)
        choices = jnp.concatenate([choice] * 8, axis=1)
        query = jnp.zeros((8, 1024), jnp.float32)
        for p in range(5):
            query = jnp.where(choices == p, queries[step, p].astype(jnp.float32)[some], query)
        query = jnp.concatenate([query[:, 128 * h:128 * h + 128] for h in range(8)], axis=0).astype(jnp.bfloat16)

        def fresh_rows(ref):
            parts = [ref[p, span, :].astype(jnp.float32)[some] for p in range(5)]
            return jnp.concatenate(parts + [blank], axis=0).astype(jnp.bfloat16)

        def scores(block):
            return lax.dot_general(query, block, (((1,), (1,)), ((), ())), preferred_element_type=jnp.float32)

        own_row = heads(row_wide)
        past = scores(keys[start])
        for i in range(1, 8):
            past = jnp.where(own_row == i, scores(keys[start + i]), past)
        past = jnp.where(heads(lane_wide < length), past * scale, -1e30)
        fresh_ok = (lane % 8 == row) & (lane // 8 <= choice) & (lane < 40)
        fresh = jnp.where(heads(fresh_ok), scores(fresh_rows(new_keys)) * scale, -1e30)
        peak = jnp.maximum(jnp.max(past, -1, keepdims=True), jnp.max(fresh, -1, keepdims=True))
        past, fresh = jnp.exp(past - peak), jnp.exp(fresh - peak)
        share = 1.0 / (jnp.sum(past, -1, keepdims=True) + jnp.sum(fresh, -1, keepdims=True))
        past, fresh = (past * share).astype(jnp.bfloat16), (fresh * share).astype(jnp.bfloat16)
        own_row = heads(row)
        mixed = jnp.dot(past, values[start], preferred_element_type=jnp.float32)
        for i in range(1, 8):
            mixed = jnp.where(own_row == i, jnp.dot(past, values[start + i], preferred_element_type=jnp.float32), mixed)
        mixed = mixed + jnp.dot(fresh, fresh_rows(new_values), preferred_element_type=jnp.float32)
        attended.append(jnp.concatenate([mixed[8 * h:8 * h + 8] for h in range(8)], axis=1))
    out[...] = jnp.concatenate(attended, axis=0).astype(jnp.bfloat16)


def exchange(lengths_hbm, accepted_hbm, queries_hbm, new_keys_hbm, new_values_hbm, keys_hbm, values_hbm, weight_hbm, out_hbm,
             lengths, accepted, queries, new_keys, new_values, keys, values, feats, weight, up_in, up_out, dn_in, dn_out, total,
             small_sem, cache_sem, load_sem, feat_sem, line_sem, cross_sem, swap_sem, up_sem, dn_sem, up_got, dn_got, store_sem):
    dp, z = lax.axis_index("dp"), lax.axis_index("tensor")
    core, chip = rem(dp, 2), div(dp, 2)
    x, y = div(chip, 4), rem(chip, 4)
    across = 1 - core

    def line_peer(k):
        return (rem(x + k * across, 4) * 4 + rem(y + k * core, 4)) * 2 + core

    def cross_peer(k):
        return (rem(x + k * core, 4) * 4 + rem(y + k * across, 4)) * 2 + core

    partner = chip * 2 + across
    above, below = (dp, rem(z + 1, 8)), (dp, rem(z + 7, 8))
    peers = [(line_peer(k), z) for k in (1, 2, 3)] + [(cross_peer(k), z) for k in (1, 2, 3)]
    peers += [(partner, z), above, below]

    smalls = [pltpu.make_async_copy(source, target, small_sem.at[i]) for i, (source, target) in enumerate(
        ((lengths_hbm, lengths), (accepted_hbm, accepted), (new_keys_hbm, new_keys), (new_values_hbm, new_values)))]

    def cache_loads(third):
        span = pl.ds(pl.multiple_of(16 * third, 16), 16)
        pairs = ((queries_hbm.at[:, span, :], queries.at[third]), (keys_hbm.at[span], keys.at[span]),
                 (values_hbm.at[span], values.at[span]))
        return [pltpu.make_async_copy(*pair, cache_sem.at[i, third]) for i, pair in enumerate(pairs)]

    weights = [pltpu.make_async_copy(weight_hbm.at[:, pl.ds(512 * h, 512)], weight.at[h], load_sem.at[h]) for h in range(2)]
    for load in smalls + cache_loads(0) + cache_loads(1) + cache_loads(2) + weights:
        load.start()

    barrier = pltpu.get_barrier_semaphore()
    for peer in peers:
        pl.semaphore_signal(barrier, inc=1, device_id=peer, device_id_type=MESH)

    def give(shard, third, to, sent):
        return pltpu.make_async_remote_copy(
            src_ref=feats.at[shard, third], dst_ref=feats.at[shard, third], send_sem=sent,
            recv_sem=feat_sem.at[shard, third], device_id=(to, z), device_id_type=MESH)

    def swap(member, third):
        return give(member * 2 + core, third, partner, swap_sem.at[member, third])

    def take(shard, third):
        give(shard, third, partner, swap_sem.at[0, 0]).wait_recv()

    odd = rem(div(y, 2) + z, 2)
    late = div(rem(2 * x + 12 - z, 8), 4)
    members = []
    for i, (even_e, odd_e) in enumerate(((0, 1), (2, 7), (6, 3), (4, 5))):
        block = rem(z + 4 + even_e + (odd_e - even_e) * odd, 8)
        members.append(across * (div(block, 2) * 4 + y) + core * (x * 4 + 2 * rem(late + i // 2, 2) + i % 2))

    def forward(i, third):
        member = members[i]

        @pl.when(member != chip)
        def _():
            take(member * 2 + core, third)
            swap(member, third).start()

        for k in (1, 3, 2):
            give(member * 2 + core, third, cross_peer(k), cross_sem.at[i, k - 1, third]).start()

    def pass_on(block, third):
        for p in range(2):
            member = 2 * block + p
            inside = across * (rem(member, 4) - y) + core * (div(member, 4) - x)

            @pl.when(inside != 0)
            def _():
                take(member * 2 + core, third)
                swap(member, third).start()

    def receive(block, third):
        for p in range(2):
            take((2 * block + p) * 2 + across, third)

    for load in smalls:
        load.wait()

    def attend_step(third, carry):
        for load in cache_loads(third):
            load.wait()
        attend_rows(third, queries, new_keys, new_values, keys, values, lengths, accepted, feats.at[dp, third])

        @pl.when(third == 0)
        def _():
            pl.semaphore_wait(barrier, len(peers))

        for k in (1, 3, 2):
            give(dp, third, line_peer(k), line_sem.at[k - 1, third]).start()
        swap(chip, third).start()

        @pl.when(third > 0)
        def _():
            forward(0, third - 1)

        return carry

    lax.fori_loop(0, 3, attend_step, 0)
    first = rem(z + 4, 8)
    forward(0, 2)
    pass_on(first, 0)

    def forward_thirds(i):
        def one(third, carry):
            forward(i, third)
            return carry
        lax.fori_loop(0, 3, one, 0)

    forward_thirds(1)
    pass_on(first, 1)
    forward_thirds(2)
    pass_on(first, 2)
    forward_thirds(3)
    for load in weights:
        load.wait()

    def send(n, goes_up):
        source, target = (up_out, up_in) if goes_up else (dn_out, dn_in)
        sent, got = (up_sem, up_got) if goes_up else (dn_sem, dn_got)
        return pltpu.make_async_remote_copy(
            src_ref=source.at[n], dst_ref=target.at[n], send_sem=sent.at[n], recv_sem=got.at[n],
            device_id=above if goes_up else below, device_id_type=MESH)

    def product(block, third, h):
        rows = feats[pl.ds(4 * block, 4), third].reshape(64, 1024)
        return jnp.dot(rows, weight[h], preferred_element_type=jnp.float32)

    def place(m):
        j = 4 - div(m, 6)
        return rem(z + j, 8), rem(z + 8 - j, 8), rem(m, 3)

    def slot(n, has_input):
        m = n + 3
        q = rem(div(m, 3), 2)
        up_block, dn_block, third = place(m)
        next_up, next_dn, next_third = place(m + 1)

        @pl.when(jnp.logical_and(rem(m + 1, 6) < 3, m < 23))
        def _():
            pass_on(next_up, next_third)
            pass_on(next_dn, next_third)

        if not has_input:
            @pl.when(m < 6)
            def _():
                receive(up_block, third)

        @pl.when(rem(m, 6) < 3)
        def _():
            receive(up_block, third)
            receive(dn_block, third)

        up = product(up_block, third, 1 - q)
        if has_input:
            send(n - 6, True).wait_recv()
            up = up + up_in[n - 6].astype(jnp.float32)
        up_out[n] = up.astype(jnp.bfloat16)
        send(n, True).start()
        dn = product(dn_block, third, q)
        if has_input:
            send(n - 6, False).wait_recv()
            dn = dn + dn_in[n - 6].astype(jnp.float32)
        dn_out[n] = dn.astype(jnp.bfloat16)
        send(n, False).start()

    def start_slot(n, carry):
        slot(n, False)
        return carry

    def inner_slot(n, carry):
        slot(n, True)
        send(n - 6, True).wait_send()
        send(n - 6, False).wait_send()
        return carry

    lax.fori_loop(0, 6, start_slot, 0)
    lax.fori_loop(6, SLOTS, inner_slot, 0)

    def own_block(third, carry):
        pass_on(z, third)
        receive(z, third)
        for h in range(2):
            total[h, third] = product(z, third, h).reshape(4, 16, 512)
        for k in (1, 2, 3):
            give(dp, third, partner, line_sem.at[k - 1, third]).wait_send()
            for i in range(4):
                give(dp, third, partner, cross_sem.at[i, k - 1, third]).wait_send()
        return carry

    lax.fori_loop(0, 3, own_block, 0)

    def drain_swap(i, carry):
        for third in range(3):
            swap(i, third).wait_send()
        return carry

    lax.fori_loop(0, 16, drain_swap, 0)

    def add_input(n, goes_up, h, third):
        send(n, goes_up).wait_recv()
        total[h, third] = total[h, third] + (up_in if goes_up else dn_in)[n].astype(jnp.float32).reshape(4, 16, 512)

    def early(third, carry):
        add_input(15 + third, True, 1, third)
        add_input(15 + third, False, 0, third)
        return carry

    lax.fori_loop(0, 3, early, 0)

    def store(h, third):
        return pltpu.make_async_copy(
            total.at[h, third],
            out_hbm.at[:, pl.ds(pl.multiple_of(16 * third, 16), 16), pl.ds(512 * h, 512)], store_sem.at[h, third])

    def ending(third, carry):
        add_input(18 + third, True, 0, third)
        store(0, third).start()
        add_input(18 + third, False, 1, third)
        store(1, third).start()
        return carry

    lax.fori_loop(0, 3, ending, 0)

    def drain(n, carry):
        send(n, True).wait_send()
        send(n, False).wait_send()
        return carry

    lax.fori_loop(15, SLOTS, drain, 0)
    for third in range(3):
        for h in range(2):
            store(h, third).wait()


def shards(queries, new_keys, new_values, key_cache, value_cache, cache_lengths, accepted, head_weight):
    dma = pltpu.SemaphoreType.DMA
    piece = pltpu.VMEM((SLOTS, 64, 512), jnp.bfloat16)
    queries, new_keys, new_values = (jnp.transpose(a, (1, 0, 2)) for a in (queries, new_keys, new_values))
    logits = pl.pallas_call(
        exchange,
        out_shape=jax.ShapeDtypeStruct((4, 48, 1024), jnp.float32),
        in_specs=[pl.BlockSpec(memory_space=pl.ANY)] * 8,
        out_specs=pl.BlockSpec(memory_space=pl.ANY),
        scratch_shapes=[
            pltpu.SMEM((48,), jnp.int32),
            pltpu.SMEM((48,), jnp.int32),
            pltpu.VMEM((3, 5, 16, 1024), jnp.bfloat16),
            pltpu.VMEM((5, 48, 128), jnp.bfloat16),
            pltpu.VMEM((5, 48, 128), jnp.bfloat16),
            pltpu.VMEM((48, 256, 128), jnp.bfloat16),
            pltpu.VMEM((48, 256, 128), jnp.bfloat16),
            pltpu.VMEM((32, 3, 16, 1024), jnp.bfloat16),
            pltpu.VMEM((2, 1024, 512), jnp.bfloat16),
            piece, piece, piece, piece,
            pltpu.VMEM((2, 3, 4, 16, 512), jnp.float32),
            dma((4,)), dma((3, 3)), dma((2,)), dma((32, 3)), dma((3, 3)), dma((4, 3, 3)), dma((16, 3)),
            dma((SLOTS,)), dma((SLOTS,)), dma((SLOTS,)), dma((SLOTS,)), dma((2, 3)),
        ],
        compiler_params=pltpu.CompilerParams(
            collective_id=0, has_side_effects=True, vmem_limit_bytes=54 * 2 ** 20),
    )(cache_lengths, accepted, queries, new_keys, new_values, key_cache, value_cache, head_weight)
    return logits.reshape(192, 1024)


def solution(mesh):
    split = P("dp", None, "tensor")
    return jax.shard_map(
        shards,
        mesh=mesh,
        in_specs=(split,) * 5 + (P("dp"), P("dp"), P("tensor", "dp")),
        out_specs=P("tensor", "dp"),
        check_vma=False,
    )
```

```python
import functools

import jax
import jax.numpy as jnp
from jax import lax
from jax.experimental import pallas as pl
from jax.experimental.pallas import tpu as pltpu
from jax.sharding import PartitionSpec as P

HEAD_DIM = 128
MESH = pl.DeviceIdType.MESH
SLOTS = 21
div, rem = lax.div, lax.rem


def attend_rows(step, queries, new_keys, new_values, keys, values, lengths, accepted, out):
    scale = HEAD_DIM ** -0.5
    row = lax.broadcasted_iota(jnp.int32, (8, 128), 0)
    lane = lax.broadcasted_iota(jnp.int32, (8, 128), 1)
    row_wide = lax.broadcasted_iota(jnp.int32, (8, 256), 0)
    lane_wide = lax.broadcasted_iota(jnp.int32, (8, 256), 1)
    blank = jnp.zeros((128 - 5 * 8, HEAD_DIM), jnp.float32)
    base = pl.multiple_of(16 * step, 16)
    span = pl.ds(base, 16)

    def heads(tile):
        return jnp.concatenate([tile] * 8, axis=0)

    attended = []
    for part in range(2):
        start, some = base + 8 * part, slice(8 * part, 8 * part + 8)
        choice = jnp.zeros((8, 128), jnp.int32)
        length = jnp.zeros((8, 256), jnp.int32)
        for i in range(8):
            choice = jnp.where(row == i, accepted[start + i], choice)
            length = jnp.where(row_wide == i, lengths[start + i], length)
        choices = jnp.concatenate([choice] * 8, axis=1)
        query = jnp.zeros((8, 1024), jnp.float32)
        for p in range(5):
            query = jnp.where(choices == p, queries[step, p].astype(jnp.float32)[some], query)
        query = jnp.concatenate([query[:, 128 * h:128 * h + 128] for h in range(8)], axis=0).astype(jnp.bfloat16)

        def fresh_rows(ref):
            parts = [ref[p, span, :].astype(jnp.float32)[some] for p in range(5)]
            return jnp.concatenate(parts + [blank], axis=0).astype(jnp.bfloat16)

        def scores(block):
            return lax.dot_general(query, block, (((1,), (1,)), ((), ())), preferred_element_type=jnp.float32)

        own_row = heads(row_wide)
        past = scores(keys[start])
        for i in range(1, 8):
            past = jnp.where(own_row == i, scores(keys[start + i]), past)
        past = jnp.where(heads(lane_wide < length), past * scale, -1e30)
        fresh_ok = (lane % 8 == row) & (lane // 8 <= choice) & (lane < 40)
        fresh = jnp.where(heads(fresh_ok), scores(fresh_rows(new_keys)) * scale, -1e30)
        peak = jnp.maximum(jnp.max(past, -1, keepdims=True), jnp.max(fresh, -1, keepdims=True))
        past, fresh = jnp.exp(past - peak), jnp.exp(fresh - peak)
        share = 1.0 / (jnp.sum(past, -1, keepdims=True) + jnp.sum(fresh, -1, keepdims=True))
        past, fresh = (past * share).astype(jnp.bfloat16), (fresh * share).astype(jnp.bfloat16)
        own_row = heads(row)
        mixed = jnp.dot(past, values[start], preferred_element_type=jnp.float32)
        for i in range(1, 8):
            mixed = jnp.where(own_row == i, jnp.dot(past, values[start + i], preferred_element_type=jnp.float32), mixed)
        mixed = mixed + jnp.dot(fresh, fresh_rows(new_values), preferred_element_type=jnp.float32)
        attended.append(jnp.concatenate([mixed[8 * h:8 * h + 8] for h in range(8)], axis=1))
    out[...] = jnp.concatenate(attended, axis=0).astype(jnp.bfloat16)


def exchange(lengths_hbm, accepted_hbm, queries_hbm, new_keys_hbm, new_values_hbm, keys_hbm, values_hbm, weight_hbm, out_hbm,
             lengths, accepted, queries, new_keys, new_values, keys, values, feats, weight, up_in, up_out, dn_in, dn_out, total,
             small_sem, cache_sem, load_sem, feat_sem, line_sem, cross_sem, swap_sem, up_sem, dn_sem, up_got, dn_got, store_sem):
    dp, z = lax.axis_index("dp"), lax.axis_index("tensor")
    core, chip = rem(dp, 2), div(dp, 2)
    x, y = div(chip, 4), rem(chip, 4)
    across = 1 - core

    def line_peer(k):
        return (rem(x + k * across, 4) * 4 + rem(y + k * core, 4)) * 2 + core

    def cross_peer(k):
        return (rem(x + k * core, 4) * 4 + rem(y + k * across, 4)) * 2 + core

    partner = chip * 2 + across
    above, below = (dp, rem(z + 1, 8)), (dp, rem(z + 7, 8))
    peers = [(line_peer(k), z) for k in (1, 2, 3)] + [(cross_peer(k), z) for k in (1, 2, 3)]
    peers += [(partner, z), above, below]

    smalls = [pltpu.make_async_copy(source, target, small_sem.at[i]) for i, (source, target) in enumerate(
        ((lengths_hbm, lengths), (accepted_hbm, accepted), (new_keys_hbm, new_keys), (new_values_hbm, new_values)))]

    def cache_loads(third):
        span = pl.ds(pl.multiple_of(16 * third, 16), 16)
        pairs = ((queries_hbm.at[:, span, :], queries.at[third]), (keys_hbm.at[span], keys.at[span]),
                 (values_hbm.at[span], values.at[span]))
        return [pltpu.make_async_copy(*pair, cache_sem.at[i, third]) for i, pair in enumerate(pairs)]

    weights = [pltpu.make_async_copy(weight_hbm.at[:, pl.ds(512 * h, 512)], weight.at[h], load_sem.at[h]) for h in range(2)]
    for load in smalls + cache_loads(0):
        load.start()

    barrier = pltpu.get_barrier_semaphore()
    for peer in peers:
        pl.semaphore_signal(barrier, inc=1, device_id=peer, device_id_type=MESH)

    def give(shard, third, to, sent):
        return pltpu.make_async_remote_copy(
            src_ref=feats.at[shard, third], dst_ref=feats.at[shard, third], send_sem=sent,
            recv_sem=feat_sem.at[shard, third], device_id=(to, z), device_id_type=MESH)

    def swap(member, third):
        return give(member * 2 + core, third, partner, swap_sem.at[member, third])

    def take(shard, third):
        give(shard, third, partner, swap_sem.at[0, 0]).wait_recv()

    odd = rem(div(y, 2) + z, 2)
    late = div(rem(2 * x + 12 - z, 8), 4)
    members = []
    for i, (even_e, odd_e) in enumerate(((0, 1), (2, 7), (6, 3), (4, 5))):
        block = rem(z + 4 + even_e + (odd_e - even_e) * odd, 8)
        members.append(across * (div(block, 2) * 4 + y) + core * (x * 4 + 2 * rem(late + i // 2, 2) + i % 2))
    first = rem(z + 4, 8)

    def stage_of(member):
        ahead = rem(div(member, 2) + 12 - z, 8)
        return jnp.minimum(ahead, 8 - ahead)


    def forward(i, third):
        member = members[i]

        @pl.when(member != chip)
        def _():
            take(member * 2 + core, third)
            swap(member, third).start()

        for k in (1, 3, 2):
            give(member * 2 + core, third, cross_peer(k), cross_sem.at[i, k - 1, third]).start()

    def forward_stage(stage, third):
        for i in range(4):
            pl.when(stage_of(members[i]) == stage)(functools.partial(forward, i, third))

    def send_line(third):
        for k in (1, 3, 2):
            give(dp, third, line_peer(k), line_sem.at[k - 1, third]).start()

    def pass_on(block, third):
        for p in range(2):
            member = 2 * block + p
            inside = across * (rem(member, 4) - y) + core * (div(member, 4) - x)

            @pl.when(inside != 0)
            def _():
                take(member * 2 + core, third)
                swap(member, third).start()

    def receive(block, third):
        for p in range(2):
            take((2 * block + p) * 2 + across, third)

    for load in smalls:
        load.wait()
    for load in cache_loads(1):
        load.start()

    def attend_step(third, carry):
        for load in cache_loads(third):
            load.wait()

        @pl.when(third == 0)
        def _():
            for load in cache_loads(2) + weights:
                load.start()

        attend_rows(third, queries, new_keys, new_values, keys, values, lengths, accepted, feats.at[dp, third])

        @pl.when(third == 0)
        def _():
            pl.semaphore_wait(barrier, len(peers))

        send_line(third)
        swap(chip, third).start()

        return carry

    lax.fori_loop(0, 3, attend_step, 0)
    forward_stage(0, 0)
    forward_stage(0, 1)
    forward_stage(1, 0)
    forward_stage(1, 1)
    forward_stage(0, 2)
    pass_on(first, 0)
    forward_stage(1, 2)
    for load in weights:
        load.wait()

    def send(n, goes_up):
        source, target = (up_out, up_in) if goes_up else (dn_out, dn_in)
        sent, got = (up_sem, up_got) if goes_up else (dn_sem, dn_got)
        return pltpu.make_async_remote_copy(
            src_ref=source.at[n], dst_ref=target.at[n], send_sem=sent.at[n], recv_sem=got.at[n],
            device_id=above if goes_up else below, device_id_type=MESH)

    def product(block, third, h):
        rows = feats[pl.ds(4 * block, 4), third].reshape(64, 1024)
        return jnp.dot(rows, weight[h], preferred_element_type=jnp.float32)

    def place(m):
        j = 4 - div(m, 6)
        return rem(z + j, 8), rem(z + 8 - j, 8), rem(m, 3)

    def slot(n, has_input):
        m = n + 3
        q = rem(div(m, 3), 2)
        up_block, dn_block, third = place(m)
        next_up, next_dn, next_third = place(m + 1)

        if not has_input:
            @pl.when(m < 6)
            def _():
                receive(up_block, third)

        @pl.when(rem(m, 6) < 3)
        def _():
            receive(up_block, third)
            receive(dn_block, third)

        up = product(up_block, third, 1 - q)
        if has_input:
            send(n - 6, True).wait_recv()
            up = up + up_in[n - 6].astype(jnp.float32)
        up_out[n] = up.astype(jnp.bfloat16)
        send(n, True).start()
        dn = product(dn_block, third, q)
        if has_input:
            send(n - 6, False).wait_recv()
            dn = dn + dn_in[n - 6].astype(jnp.float32)
        dn_out[n] = dn.astype(jnp.bfloat16)
        send(n, False).start()

        if not has_input:
            @pl.when(m < 5)
            def _():
                pass_on(first, third + 1)

            @pl.when(m < 6)
            def _():
                forward_stage(2, third)

        @pl.when(jnp.logical_and(rem(m, 6) < 3, m < 15))
        def _():
            forward_stage(div(m, 6) + 2, third)

        @pl.when(jnp.logical_and(rem(m + 1, 6) < 3, m < 23))
        def _():
            pass_on(next_up, next_third)
            pass_on(next_dn, next_third)

    def start_slot(n, carry):
        slot(n, False)
        return carry

    def inner_slot(n, carry):
        slot(n, True)
        send(n - 6, True).wait_send()
        send(n - 6, False).wait_send()
        return carry

    lax.fori_loop(0, 6, start_slot, 0)
    lax.fori_loop(6, SLOTS, inner_slot, 0)

    def own_block(third, carry):
        pass_on(z, third)
        receive(z, third)
        for h in range(2):
            total[h, third] = product(z, third, h).reshape(4, 16, 512)
        for k in (1, 2, 3):
            give(dp, third, partner, line_sem.at[k - 1, third]).wait_send()
            for i in range(4):
                give(dp, third, partner, cross_sem.at[i, k - 1, third]).wait_send()
        return carry

    lax.fori_loop(0, 3, own_block, 0)

    def drain_swap(i, carry):
        for third in range(3):
            swap(i, third).wait_send()
        return carry

    lax.fori_loop(0, 16, drain_swap, 0)

    def add_input(n, goes_up, h, third):
        send(n, goes_up).wait_recv()
        total[h, third] = total[h, third] + (up_in if goes_up else dn_in)[n].astype(jnp.float32).reshape(4, 16, 512)

    def early(third, carry):
        add_input(15 + third, True, 1, third)
        add_input(15 + third, False, 0, third)
        return carry

    lax.fori_loop(0, 3, early, 0)

    def store(h, third):
        return pltpu.make_async_copy(
            total.at[h, third],
            out_hbm.at[:, pl.ds(pl.multiple_of(16 * third, 16), 16), pl.ds(512 * h, 512)], store_sem.at[h, third])

    def ending(third, carry):
        add_input(18 + third, True, 0, third)
        store(0, third).start()
        add_input(18 + third, False, 1, third)
        store(1, third).start()
        return carry

    lax.fori_loop(0, 3, ending, 0)

    def drain(n, carry):
        send(n, True).wait_send()
        send(n, False).wait_send()
        return carry

    lax.fori_loop(15, SLOTS, drain, 0)
    for third in range(3):
        for h in range(2):
            store(h, third).wait()


def shards(queries, new_keys, new_values, key_cache, value_cache, cache_lengths, accepted, head_weight):
    dma = pltpu.SemaphoreType.DMA
    piece = pltpu.VMEM((SLOTS, 64, 512), jnp.bfloat16)
    queries, new_keys, new_values = (jnp.transpose(a, (1, 0, 2)) for a in (queries, new_keys, new_values))
    logits = pl.pallas_call(
        exchange,
        out_shape=jax.ShapeDtypeStruct((4, 48, 1024), jnp.float32),
        in_specs=[pl.BlockSpec(memory_space=pl.ANY)] * 8,
        out_specs=pl.BlockSpec(memory_space=pl.ANY),
        scratch_shapes=[
            pltpu.SMEM((48,), jnp.int32),
            pltpu.SMEM((48,), jnp.int32),
            pltpu.VMEM((3, 5, 16, 1024), jnp.bfloat16),
            pltpu.VMEM((5, 48, 128), jnp.bfloat16),
            pltpu.VMEM((5, 48, 128), jnp.bfloat16),
            pltpu.VMEM((48, 256, 128), jnp.bfloat16),
            pltpu.VMEM((48, 256, 128), jnp.bfloat16),
            pltpu.VMEM((32, 3, 16, 1024), jnp.bfloat16),
            pltpu.VMEM((2, 1024, 512), jnp.bfloat16),
            piece, piece, piece, piece,
            pltpu.VMEM((2, 3, 4, 16, 512), jnp.float32),
            dma((4,)), dma((3, 3)), dma((2,)), dma((32, 3)), dma((3, 3)), dma((4, 3, 3)), dma((16, 3)),
            dma((SLOTS,)), dma((SLOTS,)), dma((SLOTS,)), dma((SLOTS,)), dma((2, 3)),
        ],
        compiler_params=pltpu.CompilerParams(
            collective_id=0, has_side_effects=True, vmem_limit_bytes=int(52.5 * 2 ** 20)),
    )(*(pltpu.with_memory_space_constraint(a, pltpu.HBM) for a in (cache_lengths, accepted, queries, new_keys, new_values, key_cache, value_cache, head_weight)))
    return logits.reshape(192, 1024)


def solution(mesh):
    split = P("dp", None, "tensor")
    return jax.shard_map(
        shards,
        mesh=mesh,
        in_specs=(split,) * 5 + (P("dp"), P("dp"), P("tensor", "dp")),
        out_specs=P("tensor", "dp"),
        check_vma=False,
    )
```

```python
import functools

import jax
import jax.numpy as jnp
from jax import lax
from jax.experimental import pallas as pl
from jax.experimental.pallas import tpu as pltpu
from jax.sharding import PartitionSpec as P

HEAD_DIM = 128
MESH = pl.DeviceIdType.MESH
SLOTS = 21
div, rem = lax.div, lax.rem


def attend_rows(step, queries, new_keys, new_values, keys, values, lengths, accepted, out):
    scale = HEAD_DIM ** -0.5
    row = lax.broadcasted_iota(jnp.int32, (8, 128), 0)
    lane = lax.broadcasted_iota(jnp.int32, (8, 128), 1)
    row_wide = lax.broadcasted_iota(jnp.int32, (8, 256), 0)
    lane_wide = lax.broadcasted_iota(jnp.int32, (8, 256), 1)
    blank = jnp.zeros((128 - 5 * 8, HEAD_DIM), jnp.float32)
    base = pl.multiple_of(16 * step, 16)
    span = pl.ds(base, 16)

    def heads(tile):
        return jnp.concatenate([tile] * 8, axis=0)

    attended = []
    for part in range(2):
        start, some = base + 8 * part, slice(8 * part, 8 * part + 8)
        choice = jnp.zeros((8, 128), jnp.int32)
        length = jnp.zeros((8, 256), jnp.int32)
        for i in range(8):
            choice = jnp.where(row == i, accepted[start + i], choice)
            length = jnp.where(row_wide == i, lengths[start + i], length)
        choices = jnp.concatenate([choice] * 8, axis=1)
        query = jnp.zeros((8, 1024), jnp.float32)
        for p in range(5):
            query = jnp.where(choices == p, queries[step, p].astype(jnp.float32)[some], query)
        query = jnp.concatenate([query[:, 128 * h:128 * h + 128] for h in range(8)], axis=0).astype(jnp.bfloat16)

        def fresh_rows(ref):
            parts = [ref[p, span, :].astype(jnp.float32)[some] for p in range(5)]
            return jnp.concatenate(parts + [blank], axis=0).astype(jnp.bfloat16)

        def scores(block):
            return lax.dot_general(query, block, (((1,), (1,)), ((), ())), preferred_element_type=jnp.float32)

        own_row = heads(row_wide)
        past = scores(keys[start])
        for i in range(1, 8):
            past = jnp.where(own_row == i, scores(keys[start + i]), past)
        past = jnp.where(heads(lane_wide < length), past * scale, -1e30)
        fresh_ok = (lane % 8 == row) & (lane // 8 <= choice) & (lane < 40)
        fresh = jnp.where(heads(fresh_ok), scores(fresh_rows(new_keys)) * scale, -1e30)
        peak = jnp.maximum(jnp.max(past, -1, keepdims=True), jnp.max(fresh, -1, keepdims=True))
        past, fresh = jnp.exp(past - peak), jnp.exp(fresh - peak)
        share = 1.0 / (jnp.sum(past, -1, keepdims=True) + jnp.sum(fresh, -1, keepdims=True))
        past, fresh = (past * share).astype(jnp.bfloat16), (fresh * share).astype(jnp.bfloat16)
        own_row = heads(row)
        mixed = jnp.dot(past, values[start], preferred_element_type=jnp.float32)
        for i in range(1, 8):
            mixed = jnp.where(own_row == i, jnp.dot(past, values[start + i], preferred_element_type=jnp.float32), mixed)
        mixed = mixed + jnp.dot(fresh, fresh_rows(new_values), preferred_element_type=jnp.float32)
        attended.append(jnp.concatenate([mixed[8 * h:8 * h + 8] for h in range(8)], axis=1))
    out[...] = jnp.concatenate(attended, axis=0).astype(jnp.bfloat16)


def exchange(lengths_hbm, accepted_hbm, queries_hbm, new_keys_hbm, new_values_hbm, keys_hbm, values_hbm, weight_hbm, out_hbm,
             lengths, accepted, queries, new_keys, new_values, keys, values, feats, weight, up_in, up_out, dn_in, dn_out, total,
             small_sem, cache_sem, load_sem, feat_sem, line_sem, cross_sem, swap_sem, up_sem, dn_sem, up_got, dn_got, store_sem):
    dp, z = lax.axis_index("dp"), lax.axis_index("tensor")
    core, chip = rem(dp, 2), div(dp, 2)
    x, y = div(chip, 4), rem(chip, 4)
    across = 1 - core

    def line_peer(k):
        return (rem(x + k * across, 4) * 4 + rem(y + k * core, 4)) * 2 + core

    def cross_peer(k):
        return (rem(x + k * core, 4) * 4 + rem(y + k * across, 4)) * 2 + core

    partner = chip * 2 + across
    above, below = (dp, rem(z + 1, 8)), (dp, rem(z + 7, 8))
    peers = [(line_peer(k), z) for k in (1, 2, 3)] + [(cross_peer(k), z) for k in (1, 2, 3)]
    peers += [(partner, z), above, below]

    smalls = [pltpu.make_async_copy(source, target, small_sem.at[i]) for i, (source, target) in enumerate(
        ((lengths_hbm, lengths), (accepted_hbm, accepted), (new_keys_hbm, new_keys), (new_values_hbm, new_values)))]

    def cache_loads(third):
        span = pl.ds(pl.multiple_of(16 * third, 16), 16)
        pairs = ((queries_hbm.at[:, span, :], queries.at[third]), (keys_hbm.at[span], keys.at[span]),
                 (values_hbm.at[span], values.at[span]))
        return [pltpu.make_async_copy(*pair, cache_sem.at[i, third]) for i, pair in enumerate(pairs)]

    weights = [pltpu.make_async_copy(weight_hbm.at[:, pl.ds(512 * h, 512)], weight.at[h], load_sem.at[h]) for h in range(2)]
    for load in smalls + cache_loads(0):
        load.start()

    barrier = pltpu.get_barrier_semaphore()
    for peer in peers:
        pl.semaphore_signal(barrier, inc=1, device_id=peer, device_id_type=MESH)

    def give(shard, third, to, sents):
        rows, got = (feats.at[shard], 0) if third is None else (feats.at[shard, third], third)
        return pltpu.make_async_remote_copy(
            src_ref=rows, dst_ref=rows, send_sem=sents.at[got], recv_sem=feat_sem.at[shard, got],
            device_id=(to, z), device_id_type=MESH)

    def swap(member, third):
        return give(member * 2 + core, third, partner, swap_sem.at[member])

    def take(shard, third):
        give(shard, third, partner, swap_sem.at[0]).wait_recv()

    odd = rem(div(y, 2) + z, 2)
    late = div(rem(2 * x + 12 - z, 8), 4)
    members = []
    for i, (even_e, odd_e) in enumerate(((0, 1), (2, 7), (6, 3), (4, 5))):
        block = rem(z + 4 + even_e + (odd_e - even_e) * odd, 8)
        members.append(across * (div(block, 2) * 4 + y) + core * (x * 4 + 2 * rem(late + i // 2, 2) + i % 2))
    first = rem(z + 4, 8)

    def stage_of(member):
        ahead = rem(div(member, 2) + 12 - z, 8)
        return jnp.minimum(ahead, 8 - ahead)


    near = stage_of(chip) < 2

    def forward(i, third):
        member = members[i]

        @pl.when(member != chip)
        def _():
            take(member * 2 + core, third)
            swap(member, third).start()

        for k in (1, 3, 2):
            give(member * 2 + core, third, cross_peer(k), cross_sem.at[i, k - 1]).start()

    def forward_stage(stage, third):
        for i in range(4):
            pl.when(stage_of(members[i]) == stage)(functools.partial(forward, i, third))

    def send_line(third):
        for k in (1, 3, 2):
            give(dp, third, line_peer(k), line_sem.at[k - 1]).start()
        swap(chip, third).start()

    def pass_on(block, third):
        for p in range(2):
            member = 2 * block + p
            inside = across * (rem(member, 4) - y) + core * (div(member, 4) - x)

            @pl.when(inside != 0)
            def _():
                take(member * 2 + core, third)
                swap(member, third).start()

    def receive(block, third):
        for p in range(2):
            take((2 * block + p) * 2 + across, third)

    for load in smalls:
        load.wait()
    for load in cache_loads(1):
        load.start()

    def attend_step(third, carry):
        for load in cache_loads(third):
            load.wait()

        @pl.when(third == 0)
        def _():
            for load in cache_loads(2) + weights:
                load.start()

        attend_rows(third, queries, new_keys, new_values, keys, values, lengths, accepted, feats.at[dp, third])

        @pl.when(third == 0)
        def _():
            pl.semaphore_wait(barrier, len(peers))

        pl.when(near)(functools.partial(send_line, third))

        return carry

    lax.fori_loop(0, 3, attend_step, 0)
    pl.when(jnp.logical_not(near))(functools.partial(send_line, None))
    forward_stage(0, 0)
    forward_stage(0, 1)
    forward_stage(1, 0)
    forward_stage(1, 1)
    forward_stage(0, 2)
    pass_on(first, 0)
    forward_stage(1, 2)
    for load in weights:
        load.wait()

    def send(n, goes_up):
        source, target = (up_out, up_in) if goes_up else (dn_out, dn_in)
        sent, got = (up_sem, up_got) if goes_up else (dn_sem, dn_got)
        return pltpu.make_async_remote_copy(
            src_ref=source.at[n], dst_ref=target.at[n], send_sem=sent.at[n], recv_sem=got.at[n],
            device_id=above if goes_up else below, device_id_type=MESH)

    def product(block, third, h):
        rows = feats[pl.ds(4 * block, 4), third].reshape(64, 1024)
        return jnp.dot(rows, weight[h], preferred_element_type=jnp.float32)

    def place(m):
        j = 4 - div(m, 6)
        return rem(z + j, 8), rem(z + 8 - j, 8), rem(m, 3)

    def slot(n, has_input):
        m = n + 3
        q = rem(div(m, 3), 2)
        up_block, dn_block, third = place(m)

        if not has_input:
            @pl.when(m < 6)
            def _():
                receive(up_block, third)

            @pl.when(m > 5)
            def _():
                receive(up_block, third)
                receive(dn_block, third)

        else:
            @pl.when(jnp.logical_or(m == 12, m == 18))
            def _():
                receive(up_block, None)
                receive(dn_block, None)

        up = product(up_block, third, 1 - q)
        if has_input:
            send(n - 6, True).wait_recv()
            up = up + up_in[n - 6].astype(jnp.float32)
        up_out[n] = up.astype(jnp.bfloat16)
        send(n, True).start()
        dn = product(dn_block, third, q)
        if has_input:
            send(n - 6, False).wait_recv()
            dn = dn + dn_in[n - 6].astype(jnp.float32)
        dn_out[n] = dn.astype(jnp.bfloat16)
        send(n, False).start()

        if not has_input:
            @pl.when(m < 5)
            def _():
                pass_on(first, third + 1)

            @pl.when(jnp.logical_and(m > 3, m < 7))
            def _():
                pass_on(rem(z + 3, 8), m - 4)
                pass_on(rem(z + 5, 8), m - 4)

        for when, stage in ((4, 2), (7, 3), (12, 4)):
            if has_input == (when > 8):
                pl.when(m == when)(functools.partial(forward_stage, stage, None))

        if has_input:
            @pl.when(jnp.logical_or(m == 10, m == 16))
            def _():
                pass_on(rem(up_block + 7, 8), None)
                pass_on(rem(dn_block + 1, 8), None)

    def start_slot(n, carry):
        slot(n, False)
        return carry

    def inner_slot(n, carry):
        slot(n, True)
        send(n - 6, True).wait_send()
        send(n - 6, False).wait_send()
        return carry

    lax.fori_loop(0, 6, start_slot, 0)
    lax.fori_loop(6, SLOTS, inner_slot, 0)

    pass_on(z, None)
    receive(z, None)

    def own_block(third, carry):
        for h in range(2):
            total[h, third] = product(z, third, h).reshape(4, 16, 512)
        return carry

    lax.fori_loop(0, 3, own_block, 0)

    def drain(member, copies):
        def each(thirds):
            for copy in copies:
                for third in thirds:
                    copy(third).wait_send()
        pl.when(stage_of(member) < 2)(lambda: each(range(3)))
        pl.when(stage_of(member) > 1)(lambda: each([None]))

    drain(chip, [lambda third, k=k: give(dp, third, partner, line_sem.at[k]) for k in range(3)])
    for i in range(4):
        drain(members[i], [lambda third, k=k: give(dp, third, partner, cross_sem.at[i, k]) for k in range(3)])

    def drain_swap(i, carry):
        drain(i, [functools.partial(swap, i)])
        return carry

    lax.fori_loop(0, 16, drain_swap, 0)

    def add_input(n, goes_up, h, third):
        send(n, goes_up).wait_recv()
        total[h, third] = total[h, third] + (up_in if goes_up else dn_in)[n].astype(jnp.float32).reshape(4, 16, 512)

    def early(third, carry):
        add_input(15 + third, True, 1, third)
        add_input(15 + third, False, 0, third)
        return carry

    lax.fori_loop(0, 3, early, 0)

    def store(h, third):
        return pltpu.make_async_copy(
            total.at[h, third],
            out_hbm.at[:, pl.ds(pl.multiple_of(16 * third, 16), 16), pl.ds(512 * h, 512)], store_sem.at[h, third])

    def ending(third, carry):
        add_input(18 + third, True, 0, third)
        store(0, third).start()
        add_input(18 + third, False, 1, third)
        store(1, third).start()
        return carry

    lax.fori_loop(0, 3, ending, 0)

    def drain_sums(n, carry):
        send(n, True).wait_send()
        send(n, False).wait_send()
        return carry

    lax.fori_loop(15, SLOTS, drain_sums, 0)
    for third in range(3):
        for h in range(2):
            store(h, third).wait()


def shards(queries, new_keys, new_values, key_cache, value_cache, cache_lengths, accepted, head_weight):
    dma = pltpu.SemaphoreType.DMA
    piece = pltpu.VMEM((SLOTS, 64, 512), jnp.bfloat16)
    queries, new_keys, new_values = (jnp.transpose(a, (1, 0, 2)) for a in (queries, new_keys, new_values))
    logits = pl.pallas_call(
        exchange,
        out_shape=jax.ShapeDtypeStruct((4, 48, 1024), jnp.float32),
        in_specs=[pl.BlockSpec(memory_space=pl.ANY)] * 8,
        out_specs=pl.BlockSpec(memory_space=pl.ANY),
        scratch_shapes=[
            pltpu.SMEM((48,), jnp.int32),
            pltpu.SMEM((48,), jnp.int32),
            pltpu.VMEM((3, 5, 16, 1024), jnp.bfloat16),
            pltpu.VMEM((5, 48, 128), jnp.bfloat16),
            pltpu.VMEM((5, 48, 128), jnp.bfloat16),
            pltpu.VMEM((48, 256, 128), jnp.bfloat16),
            pltpu.VMEM((48, 256, 128), jnp.bfloat16),
            pltpu.VMEM((32, 3, 16, 1024), jnp.bfloat16),
            pltpu.VMEM((2, 1024, 512), jnp.bfloat16),
            piece, piece, piece, piece,
            pltpu.VMEM((2, 3, 4, 16, 512), jnp.float32),
            dma((4,)), dma((3, 3)), dma((2,)), dma((32, 3)), dma((3, 3)), dma((4, 3, 3)), dma((16, 3)),
            dma((SLOTS,)), dma((SLOTS,)), dma((SLOTS,)), dma((SLOTS,)), dma((2, 3)),
        ],
        compiler_params=pltpu.CompilerParams(
            collective_id=0, has_side_effects=True, vmem_limit_bytes=int(52.5 * 2 ** 20)),
    )(*(pltpu.with_memory_space_constraint(a, pltpu.HBM) for a in (cache_lengths, accepted, queries, new_keys, new_values, key_cache, value_cache, head_weight)))
    return logits.reshape(192, 1024)


def solution(mesh):
    split = P("dp", None, "tensor")
    return jax.shard_map(
        shards,
        mesh=mesh,
        in_specs=(split,) * 5 + (P("dp"), P("dp"), P("tensor", "dp")),
        out_specs=P("tensor", "dp"),
        check_vma=False,
    )
```

```python
import functools

import jax
import jax.numpy as jnp
from jax import lax
from jax.experimental import pallas as pl
from jax.experimental.pallas import tpu as pltpu
from jax.sharding import PartitionSpec as P

HEAD_DIM = 128
MESH = pl.DeviceIdType.MESH
SLOTS = 21
div, rem = lax.div, lax.rem


def attend_rows(step, queries, new_keys, new_values, keys, values, lengths, accepted, out, wait_values):
    scale = HEAD_DIM ** -0.5
    row = lax.broadcasted_iota(jnp.int32, (8, 128), 0)
    lane = lax.broadcasted_iota(jnp.int32, (8, 128), 1)
    row_wide = lax.broadcasted_iota(jnp.int32, (8, 256), 0)
    lane_wide = lax.broadcasted_iota(jnp.int32, (8, 256), 1)
    blank = jnp.zeros((128 - 5 * 8, HEAD_DIM), jnp.float32)
    base = pl.multiple_of(16 * step, 16)
    span = pl.ds(base, 16)

    def heads(tile):
        return jnp.concatenate([tile] * 8, axis=0)

    attended = []
    for part in range(2):
        start, some = base + 8 * part, slice(8 * part, 8 * part + 8)
        choice = jnp.zeros((8, 128), jnp.int32)
        length = jnp.zeros((8, 256), jnp.int32)
        for i in range(8):
            choice = jnp.where(row == i, accepted[start + i], choice)
            length = jnp.where(row_wide == i, lengths[start + i], length)
        choices = jnp.concatenate([choice] * 8, axis=1)
        query = jnp.zeros((8, 1024), jnp.float32)
        for p in range(5):
            query = jnp.where(choices == p, queries[step, p].astype(jnp.float32)[some], query)
        query = jnp.concatenate([query[:, 128 * h:128 * h + 128] for h in range(8)], axis=0).astype(jnp.bfloat16)

        def fresh_rows(ref):
            parts = [ref[p, span, :].astype(jnp.float32)[some] for p in range(5)]
            return jnp.concatenate(parts + [blank], axis=0).astype(jnp.bfloat16)

        def scores(block):
            return lax.dot_general(query, block, (((1,), (1,)), ((), ())), preferred_element_type=jnp.float32)

        own_row = heads(row_wide)
        past = scores(keys[start])
        for i in range(1, 8):
            past = jnp.where(own_row == i, scores(keys[start + i]), past)
        past = jnp.where(heads(lane_wide < length), past * scale, -1e30)
        fresh_ok = (lane % 8 == row) & (lane // 8 <= choice) & (lane < 40)
        fresh = jnp.where(heads(fresh_ok), scores(fresh_rows(new_keys)) * scale, -1e30)
        peak = jnp.maximum(jnp.max(past, -1, keepdims=True), jnp.max(fresh, -1, keepdims=True))
        past, fresh = jnp.exp(past - peak), jnp.exp(fresh - peak)
        share = 1.0 / (jnp.sum(past, -1, keepdims=True) + jnp.sum(fresh, -1, keepdims=True))
        past, fresh = (past * share).astype(jnp.bfloat16), (fresh * share).astype(jnp.bfloat16)
        own_row = heads(row)
        if part == 0:
            wait_values()
        mixed = jnp.dot(past, values[start], preferred_element_type=jnp.float32)
        for i in range(1, 8):
            mixed = jnp.where(own_row == i, jnp.dot(past, values[start + i], preferred_element_type=jnp.float32), mixed)
        mixed = mixed + jnp.dot(fresh, fresh_rows(new_values), preferred_element_type=jnp.float32)
        attended.append(jnp.concatenate([mixed[8 * h:8 * h + 8] for h in range(8)], axis=1))
    out[...] = jnp.concatenate(attended, axis=0).astype(jnp.bfloat16)


def exchange(lengths_hbm, accepted_hbm, queries_hbm, new_keys_hbm, new_values_hbm, keys_hbm, values_hbm, weight_hbm, logits_ref,
             lengths, accepted, queries, new_keys, new_values, keys, values, feats, weight, up_in, up_out, dn_in, dn_out,
             small_sem, cache_sem, load_sem, feat_sem, line_sem, cross_sem, swap_sem, up_sem, dn_sem, up_got, dn_got):
    dp, z = lax.axis_index("dp"), lax.axis_index("tensor")
    core, chip = rem(dp, 2), div(dp, 2)
    x, y = div(chip, 4), rem(chip, 4)
    across = 1 - core

    def line_peer(k):
        return (rem(x + k * across, 4) * 4 + rem(y + k * core, 4)) * 2 + core

    def cross_peer(k):
        return (rem(x + k * core, 4) * 4 + rem(y + k * across, 4)) * 2 + core

    partner = chip * 2 + across
    above, below = (dp, rem(z + 1, 8)), (dp, rem(z + 7, 8))
    peers = [(line_peer(k), z) for k in (1, 2, 3)] + [(cross_peer(k), z) for k in (1, 2, 3)]
    peers += [(partner, z), above, below]

    smalls = [pltpu.make_async_copy(source, target, small_sem.at[i]) for i, (source, target) in enumerate(
        ((lengths_hbm, lengths), (accepted_hbm, accepted), (new_keys_hbm, new_keys), (new_values_hbm, new_values)))]

    def cache_loads(third):
        span = pl.ds(pl.multiple_of(16 * third, 16), 16)
        pairs = ((queries_hbm.at[:, span, :], queries.at[third]), (keys_hbm.at[span], keys.at[span]),
                 (values_hbm.at[span], values.at[span]))
        return [pltpu.make_async_copy(*pair, cache_sem.at[i, third]) for i, pair in enumerate(pairs)]

    weights = [pltpu.make_async_copy(weight_hbm.at[:, pl.ds(512 * h, 512)], weight.at[h], load_sem.at[h]) for h in range(2)]
    for load in smalls + cache_loads(0):
        load.start()

    barrier = pltpu.get_barrier_semaphore()
    for peer in peers:
        pl.semaphore_signal(barrier, inc=1, device_id=peer, device_id_type=MESH)

    def give(shard, third, to, sents):
        rows, got = (feats.at[shard], 0) if third is None else (feats.at[shard, third], third)
        return pltpu.make_async_remote_copy(
            src_ref=rows, dst_ref=rows, send_sem=sents.at[got], recv_sem=feat_sem.at[shard, got],
            device_id=(to, z), device_id_type=MESH)

    def swap(member, third):
        return give(member * 2 + core, third, partner, swap_sem.at[member])

    def take(shard, third):
        give(shard, third, partner, swap_sem.at[0]).wait_recv()

    odd = rem(div(y, 2) + z, 2)
    late = div(rem(2 * x + 12 - z, 8), 4)
    members = []
    for i, (even_e, odd_e) in enumerate(((0, 1), (2, 7), (6, 3), (4, 5))):
        block = rem(z + 4 + even_e + (odd_e - even_e) * odd, 8)
        members.append(across * (div(block, 2) * 4 + y) + core * (x * 4 + 2 * rem(late + i // 2, 2) + i % 2))
    first = rem(z + 4, 8)

    def stage_of(member):
        ahead = rem(div(member, 2) + 12 - z, 8)
        return jnp.minimum(ahead, 8 - ahead)


    near = stage_of(chip) < 2

    def forward(i, third):
        member = members[i]

        @pl.when(member != chip)
        def _():
            take(member * 2 + core, third)
            swap(member, third).start()

        for k in (1, 3, 2):
            give(member * 2 + core, third, cross_peer(k), cross_sem.at[i, k - 1]).start()

    def forward_stage(stage, third):
        for i in range(4):
            pl.when(stage_of(members[i]) == stage)(functools.partial(forward, i, third))

    def send_line(third):
        for k in (1, 3, 2):
            give(dp, third, line_peer(k), line_sem.at[k - 1]).start()
        swap(chip, third).start()

    def pass_on(block, third):
        for p in range(2):
            member = 2 * block + p
            inside = across * (rem(member, 4) - y) + core * (div(member, 4) - x)

            @pl.when(inside != 0)
            def _():
                take(member * 2 + core, third)
                swap(member, third).start()

    def receive(block, third):
        for p in range(2):
            take((2 * block + p) * 2 + across, third)

    for load in smalls:
        load.wait()
    for load in cache_loads(1):
        load.start()

    def attend_step(third, carry):
        *ahead, last = cache_loads(third)
        for load in ahead:
            load.wait()

        @pl.when(third == 0)
        def _():
            for load in cache_loads(2) + weights:
                load.start()

        attend_rows(third, queries, new_keys, new_values, keys, values, lengths, accepted, feats.at[dp, third],
                    last.wait)

        @pl.when(third == 0)
        def _():
            pl.semaphore_wait(barrier, len(peers))

        pl.when(near)(functools.partial(send_line, third))

        return carry

    lax.fori_loop(0, 3, attend_step, 0)
    pl.when(jnp.logical_not(near))(functools.partial(send_line, None))
    forward_stage(0, 0)
    forward_stage(0, 1)
    forward_stage(0, 2)
    forward_stage(1, 0)
    forward_stage(1, 1)
    pass_on(first, 0)
    forward_stage(1, 2)
    forward_stage(2, None)
    for load in weights:
        load.wait()

    def send(n, goes_up):
        source, target = (up_out, up_in) if goes_up else (dn_out, dn_in)
        sent, got = (up_sem, up_got) if goes_up else (dn_sem, dn_got)
        return pltpu.make_async_remote_copy(
            src_ref=source.at[n], dst_ref=target.at[n], send_sem=sent.at[n], recv_sem=got.at[n],
            device_id=above if goes_up else below, device_id_type=MESH)

    def product(block, third, h):
        rows = feats[pl.ds(4 * block, 4), third].reshape(64, 1024)
        return jnp.dot(rows, weight[h], preferred_element_type=jnp.float32)

    def place(m):
        j = 4 - div(m, 6)
        return rem(z + j, 8), rem(z + 8 - j, 8), rem(m, 3)

    def slot(n, has_input):
        m = n + 3
        q = rem(div(m, 3), 2)
        up_block, dn_block, third = place(m)

        if not has_input:
            @pl.when(m < 6)
            def _():
                receive(up_block, third)

            @pl.when(m > 5)
            def _():
                receive(up_block, third)
                receive(dn_block, third)

        else:
            @pl.when(jnp.logical_or(m == 12, m == 18))
            def _():
                receive(up_block, None)
                receive(dn_block, None)

        up = product(up_block, third, 1 - q)
        if has_input:
            send(n - 6, True).wait_recv()
            up = up + up_in[n - 6].astype(jnp.float32)
        up_out[n] = up.astype(jnp.bfloat16)
        send(n, True).start()
        dn = product(dn_block, third, q)
        if has_input:
            send(n - 6, False).wait_recv()
            dn = dn + dn_in[n - 6].astype(jnp.float32)
        dn_out[n] = dn.astype(jnp.bfloat16)
        send(n, False).start()

        if not has_input:
            @pl.when(m < 5)
            def _():
                pass_on(first, third + 1)

            @pl.when(jnp.logical_and(m > 3, m < 7))
            def _():
                pass_on(rem(z + 3, 8), m - 4)
                pass_on(rem(z + 5, 8), m - 4)

        for when, stage in ((4, 3), (8, 4)):
            if has_input == (when > 8):
                pl.when(m == when)(functools.partial(forward_stage, stage, None))

        if has_input:
            @pl.when(jnp.logical_or(m == 10, m == 16))
            def _():
                pass_on(rem(up_block + 7, 8), None)
                pass_on(rem(dn_block + 1, 8), None)

    def start_slot(n, carry):
        slot(n, False)
        return carry

    def inner_slot(n, carry):
        slot(n, True)
        send(n - 6, True).wait_send()
        send(n - 6, False).wait_send()
        return carry

    lax.fori_loop(0, 6, start_slot, 0)
    lax.fori_loop(6, SLOTS, inner_slot, 0)

    pass_on(z, None)
    receive(z, None)

    def spot(h, third):
        return slice(None), pl.ds(pl.multiple_of(16 * third, 16), 16), slice(512 * h, 512 * h + 512)

    def own_block(third, carry):
        for h in range(2):
            logits_ref[spot(h, third)] = product(z, third, h).reshape(4, 16, 512)
        return carry

    lax.fori_loop(0, 3, own_block, 0)

    def drain(member, copies):
        def each(thirds):
            for copy in copies:
                for third in thirds:
                    copy(third).wait_send()
        pl.when(stage_of(member) < 2)(lambda: each(range(3)))
        pl.when(stage_of(member) > 1)(lambda: each([None]))

    drain(chip, [lambda third, k=k: give(dp, third, partner, line_sem.at[k]) for k in range(3)])
    for i in range(4):
        drain(members[i], [lambda third, k=k: give(dp, third, partner, cross_sem.at[i, k]) for k in range(3)])

    def drain_swap(i, carry):
        drain(i, [functools.partial(swap, i)])
        return carry

    lax.fori_loop(0, 16, drain_swap, 0)

    def add_input(n, goes_up, h, third):
        send(n, goes_up).wait_recv()
        logits_ref[spot(h, third)] = logits_ref[spot(h, third)] + (up_in if goes_up else dn_in)[n].astype(jnp.float32).reshape(4, 16, 512)

    def early(third, carry):
        add_input(15 + third, True, 1, third)
        add_input(15 + third, False, 0, third)
        return carry

    lax.fori_loop(0, 3, early, 0)

    def ending(third, carry):
        add_input(18 + third, True, 0, third)
        add_input(18 + third, False, 1, third)
        return carry

    lax.fori_loop(0, 3, ending, 0)

    def drain_sums(n, carry):
        send(n, True).wait_send()
        send(n, False).wait_send()
        return carry

    lax.fori_loop(15, SLOTS, drain_sums, 0)


def shards(queries, new_keys, new_values, key_cache, value_cache, cache_lengths, accepted, head_weight):
    dma = pltpu.SemaphoreType.DMA
    piece = pltpu.VMEM((SLOTS, 64, 512), jnp.bfloat16)
    queries, new_keys, new_values = (jnp.transpose(a, (1, 0, 2)) for a in (queries, new_keys, new_values))
    logits = pl.pallas_call(
        exchange,
        out_shape=jax.ShapeDtypeStruct((4, 48, 1024), jnp.float32),
        in_specs=[pl.BlockSpec(memory_space=pl.ANY)] * 8,
        out_specs=pl.BlockSpec(memory_space=pltpu.VMEM),
        scratch_shapes=[
            pltpu.SMEM((48,), jnp.int32),
            pltpu.SMEM((48,), jnp.int32),
            pltpu.VMEM((3, 5, 16, 1024), jnp.bfloat16),
            pltpu.VMEM((5, 48, 128), jnp.bfloat16),
            pltpu.VMEM((5, 48, 128), jnp.bfloat16),
            pltpu.VMEM((48, 256, 128), jnp.bfloat16),
            pltpu.VMEM((48, 256, 128), jnp.bfloat16),
            pltpu.VMEM((32, 3, 16, 1024), jnp.bfloat16),
            pltpu.VMEM((2, 1024, 512), jnp.bfloat16),
            piece, piece, piece, piece,
            dma((4,)), dma((3, 3)), dma((2,)), dma((32, 3)), dma((3, 3)), dma((4, 3, 3)), dma((16, 3)),
            dma((SLOTS,)), dma((SLOTS,)), dma((SLOTS,)), dma((SLOTS,)),
        ],
        compiler_params=pltpu.CompilerParams(
            collective_id=0, has_side_effects=True, vmem_limit_bytes=int(52.5 * 2 ** 20)),
    )(*(pltpu.with_memory_space_constraint(a, pltpu.HBM) for a in (cache_lengths, accepted, queries, new_keys, new_values, key_cache, value_cache, head_weight)))
    return logits.reshape(192, 1024)


def solution(mesh):
    split = P("dp", None, "tensor")
    return jax.shard_map(
        shards,
        mesh=mesh,
        in_specs=(split,) * 5 + (P("dp"), P("dp"), P("tensor", "dp")),
        out_specs=P("tensor", "dp"),
        check_vma=False,
    )
```

```python
import functools

import jax
import jax.numpy as jnp
from jax import lax
from jax.experimental import pallas as pl
from jax.experimental.pallas import tpu as pltpu
from jax.sharding import PartitionSpec as P

HEAD_DIM = 128
MESH = pl.DeviceIdType.MESH
SLOTS = 21
div, rem = lax.div, lax.rem


def attend_rows(step, queries, new_keys, new_values, keys, values, lengths, accepted, out, wait_values):
    scale = HEAD_DIM ** -0.5
    row = lax.broadcasted_iota(jnp.int32, (8, 128), 0)
    lane = lax.broadcasted_iota(jnp.int32, (8, 128), 1)
    row_wide = lax.broadcasted_iota(jnp.int32, (8, 256), 0)
    lane_wide = lax.broadcasted_iota(jnp.int32, (8, 256), 1)
    blank = jnp.zeros((128 - 5 * 8, HEAD_DIM), jnp.float32)
    base = pl.multiple_of(16 * step, 16)
    span = pl.ds(base, 16)

    def heads(tile):
        return jnp.concatenate([tile] * 8, axis=0)

    attended = []
    for part in range(2):
        start, some = base + 8 * part, slice(8 * part, 8 * part + 8)
        choice = jnp.zeros((8, 128), jnp.int32)
        length = jnp.zeros((8, 256), jnp.int32)
        for i in range(8):
            choice = jnp.where(row == i, accepted[start + i], choice)
            length = jnp.where(row_wide == i, lengths[start + i], length)
        choices = jnp.concatenate([choice] * 8, axis=1)
        query = jnp.zeros((8, 1024), jnp.float32)
        for p in range(5):
            query = jnp.where(choices == p, queries[step, p].astype(jnp.float32)[some], query)
        query = jnp.concatenate([query[:, 128 * h:128 * h + 128] for h in range(8)], axis=0).astype(jnp.bfloat16)

        def fresh_rows(ref):
            parts = [ref[p, span, :].astype(jnp.float32)[some] for p in range(5)]
            return jnp.concatenate(parts + [blank], axis=0).astype(jnp.bfloat16)

        def scores(block):
            return lax.dot_general(query, block, (((1,), (1,)), ((), ())), preferred_element_type=jnp.float32)

        own_row = heads(row_wide)
        past = scores(keys[start])
        for i in range(1, 8):
            past = jnp.where(own_row == i, scores(keys[start + i]), past)
        past = jnp.where(heads(lane_wide < length), past * scale, -1e30)
        fresh_ok = (lane % 8 == row) & (lane // 8 <= choice) & (lane < 40)
        fresh = jnp.where(heads(fresh_ok), scores(fresh_rows(new_keys)) * scale, -1e30)
        peak = jnp.maximum(jnp.max(past, -1, keepdims=True), jnp.max(fresh, -1, keepdims=True))
        past, fresh = jnp.exp(past - peak), jnp.exp(fresh - peak)
        share = 1.0 / (jnp.sum(past, -1, keepdims=True) + jnp.sum(fresh, -1, keepdims=True))
        past, fresh = (past * share).astype(jnp.bfloat16), (fresh * share).astype(jnp.bfloat16)
        own_row = heads(row)
        if part == 0:
            wait_values()
        mixed = jnp.dot(past, values[start], preferred_element_type=jnp.float32)
        for i in range(1, 8):
            mixed = jnp.where(own_row == i, jnp.dot(past, values[start + i], preferred_element_type=jnp.float32), mixed)
        mixed = mixed + jnp.dot(fresh, fresh_rows(new_values), preferred_element_type=jnp.float32)
        attended.append(jnp.concatenate([mixed[8 * h:8 * h + 8] for h in range(8)], axis=1))
    out[...] = jnp.concatenate(attended, axis=0).astype(jnp.bfloat16)


def exchange(lengths_hbm, accepted_hbm, queries_hbm, new_keys_hbm, new_values_hbm, keys_hbm, values_hbm, weight_hbm, logits_ref,
             lengths, accepted, queries, new_keys, new_values, keys, values, feats, weight, up_in, up_out, dn_in, dn_out,
             small_sem, cache_sem, load_sem, feat_sem, line_sem, cross_sem, swap_sem, up_sem, dn_sem, up_got, dn_got):
    dp, z = lax.axis_index("dp"), lax.axis_index("tensor")
    core, chip = rem(dp, 2), div(dp, 2)
    x, y = div(chip, 4), rem(chip, 4)
    across = 1 - core

    def line_peer(k):
        return (rem(x + k * across, 4) * 4 + rem(y + k * core, 4)) * 2 + core

    def cross_peer(k):
        return (rem(x + k * core, 4) * 4 + rem(y + k * across, 4)) * 2 + core

    partner = chip * 2 + across
    above, below = (dp, rem(z + 1, 8)), (dp, rem(z + 7, 8))
    peers = [(line_peer(k), z) for k in (1, 2, 3)] + [(cross_peer(k), z) for k in (1, 2, 3)]
    peers += [(partner, z), above, below]

    smalls = [pltpu.make_async_copy(source, target, small_sem.at[i]) for i, (source, target) in enumerate(
        ((lengths_hbm, lengths), (accepted_hbm, accepted), (new_keys_hbm, new_keys), (new_values_hbm, new_values)))]

    def cache_loads(third):
        span = pl.ds(pl.multiple_of(16 * third, 16), 16)
        pairs = ((queries_hbm.at[:, span, :], queries.at[third]), (keys_hbm.at[span], keys.at[span]),
                 (values_hbm.at[span], values.at[span]))
        return [pltpu.make_async_copy(*pair, cache_sem.at[i, third]) for i, pair in enumerate(pairs)]

    weights = [pltpu.make_async_copy(weight_hbm.at[:, pl.ds(512 * h, 512)], weight.at[h], load_sem.at[h]) for h in range(2)]
    for load in smalls + cache_loads(0):
        load.start()

    barrier = pltpu.get_barrier_semaphore()
    for peer in peers:
        pl.semaphore_signal(barrier, inc=1, device_id=peer, device_id_type=MESH)

    def give(shard, third, to, sents):
        rows, got = (feats.at[shard], 0) if third is None else (feats.at[shard, third], third)
        return pltpu.make_async_remote_copy(
            src_ref=rows, dst_ref=rows, send_sem=sents.at[got], recv_sem=feat_sem.at[shard, got],
            device_id=(to, z), device_id_type=MESH)

    def swap(member, third):
        return give(member * 2 + core, third, partner, swap_sem.at[member])

    def take(shard, third):
        give(shard, third, partner, swap_sem.at[0]).wait_recv()

    odd = rem(div(y, 2) + z, 2)
    late = div(rem(2 * x + 12 - z, 8), 4)
    members = []
    for i, (even_e, odd_e) in enumerate(((0, 1), (2, 7), (6, 3), (4, 5))):
        block = rem(z + 4 + even_e + (odd_e - even_e) * odd, 8)
        members.append(across * (div(block, 2) * 4 + y) + core * (x * 4 + 2 * rem(late + i // 2, 2) + i % 2))
    first = rem(z + 4, 8)

    def stage_of(member):
        ahead = rem(div(member, 2) + 12 - z, 8)
        return jnp.minimum(ahead, 8 - ahead)


    near = stage_of(chip) < 2

    def forward(i, third):
        member = members[i]

        @pl.when(member != chip)
        def _():
            take(member * 2 + core, third)
            swap(member, third).start()

        for k in (1, 3, 2):
            give(member * 2 + core, third, cross_peer(k), cross_sem.at[i, k - 1]).start()

    def forward_stage(stage, third):
        for i in range(4):
            pl.when(stage_of(members[i]) == stage)(functools.partial(forward, i, third))

    def send_line(third):
        for k in (1, 3, 2):
            give(dp, third, line_peer(k), line_sem.at[k - 1]).start()
        swap(chip, third).start()

    def pass_on(block, third):
        for p in range(2):
            member = 2 * block + p
            inside = across * (rem(member, 4) - y) + core * (div(member, 4) - x)

            @pl.when(inside != 0)
            def _():
                take(member * 2 + core, third)
                swap(member, third).start()

    def receive(block, third):
        for p in range(2):
            take((2 * block + p) * 2 + across, third)

    for load in smalls:
        load.wait()
    for load in cache_loads(1):
        load.start()

    def attend_step(third, carry):
        *ahead, last = cache_loads(third)
        for load in ahead:
            load.wait()

        @pl.when(third == 0)
        def _():
            for load in cache_loads(2) + weights:
                load.start()

        attend_rows(third, queries, new_keys, new_values, keys, values, lengths, accepted, feats.at[dp, third],
                    last.wait)

        @pl.when(third == 0)
        def _():
            pl.semaphore_wait(barrier, len(peers))

        pl.when(near)(functools.partial(send_line, third))

        return carry

    lax.fori_loop(0, 3, attend_step, 0)
    pl.when(jnp.logical_not(near))(functools.partial(send_line, None))
    forward_stage(0, 0)
    forward_stage(0, 1)
    forward_stage(0, 2)
    forward_stage(1, 0)
    forward_stage(1, 1)
    pass_on(first, 0)
    forward_stage(1, 2)
    forward_stage(2, None)
    for load in weights:
        load.wait()

    def send(n, goes_up):
        source, target = (up_out, up_in) if goes_up else (dn_out, dn_in)
        sent, got = (up_sem, up_got) if goes_up else (dn_sem, dn_got)
        return pltpu.make_async_remote_copy(
            src_ref=source.at[n], dst_ref=target.at[n], send_sem=sent.at[n], recv_sem=got.at[n],
            device_id=above if goes_up else below, device_id_type=MESH)

    def product(block, third, h):
        rows = feats[pl.ds(4 * block, 4), third].reshape(64, 1024)
        return jnp.dot(rows, weight[h], preferred_element_type=jnp.float32)

    def place(m):
        j = 4 - div(m, 6)
        return rem(z + j, 8), rem(z + 8 - j, 8), rem(m, 3)

    def slot(n, has_input):
        m = n + 3
        q = rem(div(m, 3), 2)
        up_block, dn_block, third = place(m)

        if not has_input:
            @pl.when(m < 6)
            def _():
                receive(up_block, third)

            @pl.when(m > 5)
            def _():
                receive(up_block, third)
                receive(dn_block, third)

        else:
            @pl.when(jnp.logical_or(m == 12, m == 18))
            def _():
                receive(up_block, None)
                receive(dn_block, None)

        up, dn = product(up_block, third, 1 - q), product(dn_block, third, q)
        if has_input:
            send(n - 6, True).wait_recv()
            up = up + up_in[n - 6].astype(jnp.float32)
        up_out[n] = up.astype(jnp.bfloat16)
        send(n, True).start()
        if has_input:
            send(n - 6, False).wait_recv()
            dn = dn + dn_in[n - 6].astype(jnp.float32)
        dn_out[n] = dn.astype(jnp.bfloat16)
        send(n, False).start()

        if not has_input:
            @pl.when(m < 5)
            def _():
                pass_on(first, third + 1)

            @pl.when(jnp.logical_and(m > 3, m < 7))
            def _():
                pass_on(rem(z + 3, 8), m - 4)
                pass_on(rem(z + 5, 8), m - 4)

        for when, stage in ((4, 3), (8, 4)):
            if has_input == (when > 8):
                pl.when(m == when)(functools.partial(forward_stage, stage, None))

        if has_input:
            @pl.when(jnp.logical_or(m == 10, m == 16))
            def _():
                pass_on(rem(up_block + 7, 8), None)
                pass_on(rem(dn_block + 1, 8), None)

    def start_slot(n, carry):
        slot(n, False)
        return carry

    def inner_slot(n, carry):
        slot(n, True)
        return carry

    lax.fori_loop(0, 6, start_slot, 0)
    lax.fori_loop(6, SLOTS, inner_slot, 0)

    pass_on(z, None)
    receive(z, None)

    def spot(h, third):
        return slice(None), pl.ds(pl.multiple_of(16 * third, 16), 16), slice(512 * h, 512 * h + 512)

    def own_block(third, carry):
        for h in range(2):
            logits_ref[spot(h, third)] = product(z, third, h).reshape(4, 16, 512)
        return carry

    lax.fori_loop(0, 3, own_block, 0)

    def drain(member, copies):
        def each(thirds):
            for copy in copies:
                for third in thirds:
                    copy(third).wait_send()
        pl.when(stage_of(member) < 2)(lambda: each(range(3)))
        pl.when(stage_of(member) > 1)(lambda: each([None]))

    drain(chip, [lambda third, k=k: give(dp, third, partner, line_sem.at[k]) for k in range(3)])
    for i in range(4):
        drain(members[i], [lambda third, k=k: give(dp, third, partner, cross_sem.at[i, k]) for k in range(3)])

    def drain_swap(i, carry):
        drain(i, [functools.partial(swap, i)])
        return carry

    lax.fori_loop(0, 16, drain_swap, 0)

    def drain_early(n, carry):
        send(n, True).wait_send()
        send(n, False).wait_send()
        return carry

    lax.fori_loop(0, 15, drain_early, 0)

    def add_input(n, goes_up, h, third):
        send(n, goes_up).wait_recv()
        logits_ref[spot(h, third)] = logits_ref[spot(h, third)] + (up_in if goes_up else dn_in)[n].astype(jnp.float32).reshape(4, 16, 512)

    def early(third, carry):
        add_input(15 + third, True, 1, third)
        add_input(15 + third, False, 0, third)
        return carry

    lax.fori_loop(0, 3, early, 0)

    def ending(third, carry):
        add_input(18 + third, True, 0, third)
        add_input(18 + third, False, 1, third)
        return carry

    lax.fori_loop(0, 3, ending, 0)

    def drain_sums(n, carry):
        send(n, True).wait_send()
        send(n, False).wait_send()
        return carry

    lax.fori_loop(15, SLOTS, drain_sums, 0)


def shards(queries, new_keys, new_values, key_cache, value_cache, cache_lengths, accepted, head_weight):
    dma = pltpu.SemaphoreType.DMA
    piece = pltpu.VMEM((SLOTS, 64, 512), jnp.bfloat16)
    queries, new_keys, new_values = (jnp.transpose(a, (1, 0, 2)) for a in (queries, new_keys, new_values))
    logits = pl.pallas_call(
        exchange,
        out_shape=jax.ShapeDtypeStruct((4, 48, 1024), jnp.float32),
        in_specs=[pl.BlockSpec(memory_space=pl.ANY)] * 8,
        out_specs=pl.BlockSpec(memory_space=pltpu.VMEM),
        scratch_shapes=[
            pltpu.SMEM((48,), jnp.int32),
            pltpu.SMEM((48,), jnp.int32),
            pltpu.VMEM((3, 5, 16, 1024), jnp.bfloat16),
            pltpu.VMEM((5, 48, 128), jnp.bfloat16),
            pltpu.VMEM((5, 48, 128), jnp.bfloat16),
            pltpu.VMEM((48, 256, 128), jnp.bfloat16),
            pltpu.VMEM((48, 256, 128), jnp.bfloat16),
            pltpu.VMEM((32, 3, 16, 1024), jnp.bfloat16),
            pltpu.VMEM((2, 1024, 512), jnp.bfloat16),
            piece, piece, piece, piece,
            dma((4,)), dma((3, 3)), dma((2,)), dma((32, 3)), dma((3, 3)), dma((4, 3, 3)), dma((16, 3)),
            dma((SLOTS,)), dma((SLOTS,)), dma((SLOTS,)), dma((SLOTS,)),
        ],
        compiler_params=pltpu.CompilerParams(
            collective_id=0, has_side_effects=True, vmem_limit_bytes=int(52.5 * 2 ** 20)),
    )(*(pltpu.with_memory_space_constraint(a, pltpu.HBM) for a in (cache_lengths, accepted, queries, new_keys, new_values, key_cache, value_cache, head_weight)))
    return logits.reshape(192, 1024)


def solution(mesh):
    split = P("dp", None, "tensor")
    return jax.shard_map(
        shards,
        mesh=mesh,
        in_specs=(split,) * 5 + (P("dp"), P("dp"), P("tensor", "dp")),
        out_specs=P("tensor", "dp"),
        check_vma=False,
    )
```
